128 devices in a mesh: rad: 8 (over z, x_hi), azi: 16 (over x_lo, y, core).
Axes of the slice: x: 4 (x_hi: 2, x_lo: 2; x = x_hi * 2 + x_lo), y: 4, z: 4, core: 2. Of those that a mesh axis runs over, the one named last changes fastest.
Arguments:
- fields: float32 [8, 2, 512, 8192], P(None, None, 'rad', 'azi'), may hold values from -6 to 6
- offsets: int32 [2, 512], P(None, 'rad'), may hold values from 0 to 8191
- fractions: float32 [2, 512], P(None, 'rad'), may hold values from 0 to 1
- coefs: float32 [512], P('rad'), may hold values from 0.02 to 0.3
Outputs:
- advanced: float32 [8, 2, 512, 8192], P(None, None, 'rad', 'azi')
The draws below stay inside these ranges and needn't reach their ends.
All inputs are finite; a program needn't handle non-finite values.
Results may differ from the reference program's by a relative error of at most 0.00002.
Values sent between devices are 32-bit elements; how exact they have to be, the bound alone decides.
No kernel may reach another device: no remote copies, remote signals or barrier semaphores. Data moves between devices by JAX's collectives and lax.ppermute only.
A program may use at most 128 MiB of HBM per device.

```python
import math
import jax
import jax.numpy as jnp

FIELDS = 8
LAYERS = 2
STEPS = 2
NR = 512
NPHI = 8192


def with_ends(values, rng, least, top_value):
    shape = values.shape
    index_at = [jax.random.randint(jax.random.fold_in(rng, axis), (), 0, shape[axis]) for axis in range(len(shape))]
    values = values.at[tuple(index_at)].set(least)
    longest = shape.index(max(shape))
    index_at[longest] = (index_at[longest] + 1) % shape[longest]
    return values.at[tuple(index_at)].set(top_value)


def block_scale(own_key, shape, shards, low, high):
    gain, own = 1.0, jax.random.fold_in(own_key, 6)
    for dim, parts in shards:
        steps = jnp.exp(jax.random.uniform(jax.random.fold_in(own, dim), (parts,), jnp.float32, low / len(shards), high / len(shards)))
        gain = gain * jnp.repeat(steps, shape[dim] // parts).reshape([-1 if axis == dim else 1 for axis in range(len(shape))])
    return gain


def normal_values(stream_key, dims, spread, reach, cuts=(), held_as=jnp.bfloat16):
    factor_of = block_scale(stream_key, dims, cuts, -0.22, 0.18) if cuts else 1.0
    array = jax.random.normal(stream_key, dims, jnp.float32) * spread * factor_of
    return jnp.minimum(jnp.maximum(array, -reach), reach).astype(held_as)


def setup_inputs(seed: int = 0) -> dict:
    arg_keys = jax.random.split(jax.random.key(seed), 5)
    return {
        "fields": normal_values(arg_keys[0], (FIELDS, LAYERS, NR, NPHI), 1.0, 6.0, ((2, 8), (3, 16)), jnp.float32),
        "offsets": with_ends(jax.random.randint(arg_keys[1], (STEPS, NR), 0, NPHI), jax.random.fold_in(arg_keys[1], 1), 0, NPHI - 1).astype(jnp.int32),
        "fractions": jnp.clip(1.0 * jax.random.uniform(arg_keys[2], (STEPS, NR), jnp.float32) ** block_scale(arg_keys[2], (STEPS, NR), ((1, 8),), -0.2, 0.2), 0.0, 1.0),
        "coefs": jnp.clip(jnp.exp(math.log(0.3) - 2.7080503 * jax.random.uniform(arg_keys[3], (NR,), jnp.float32) ** block_scale(arg_keys[3], (NR,), ((0, 8),), -0.2, 0.2)), 0.02, 0.3),
    }


def reference(fields, offsets, fractions, coefs):
    state = fields
    cells = jnp.arange(NPHI, dtype=jnp.int32)
    radii = jnp.arange(NR, dtype=jnp.int32)[:, None]
    for section in range(STEPS):
        padded = jnp.pad(state, ((0, 0), (0, 0), (2, 2), (0, 0)))
        second = (16.0 * (padded[:, :, 1:-3] + padded[:, :, 3:-1]) - (padded[:, :, :-4] + padded[:, :, 4:]) - 30.0 * state) / 12.0
        state = state + coefs[:, None] * second
        shifts = offsets[section][:, None]
        source = jnp.mod(cells[None, :] - shifts, NPHI).astype(jnp.int32)
        source_next = jnp.mod(cells[None, :] - shifts - 1, NPHI).astype(jnp.int32)
        weight = fractions[section][:, None]
        first = state[:, :, radii, source]
        behind = state[:, :, radii, source_next]
        state = (1.0 - weight) * first + weight * behind
    return state
```

```python
import functools

import jax
import jax.numpy as jnp
from jax import lax
from jax.experimental import pallas as pl
from jax.experimental.pallas import tpu as pltpu
from jax.sharding import PartitionSpec as P

LANES = 128
HALO = 4


def diffused(far_up, up, here, down, far_down, factor):
    return here + factor * (16.0 * (up + down) - (far_up + far_down) - 30.0 * here)


def partly_shifted(row, shift, weight, carry_ref):
    lines = row.shape[0]
    part = shift & (LANES - 1)
    lane = lax.broadcasted_iota(jnp.int32, row.shape, 1)
    first = (1.0 - weight) * pltpu.roll(row, part, 1)
    behind = weight * pltpu.roll(row, (part + 1) & (LANES - 1), 1)
    stays_first = lane >= part
    stays_behind = lane > part
    stays = jnp.where(stays_first, first, 0.0) + jnp.where(stays_behind, behind, 0.0)
    moves = jnp.where(stays_first, 0.0, first) + jnp.where(stays_behind, 0.0, behind)
    carry_ref[pl.ds(8, lines)] = moves
    carry_ref[pl.ds(7, 1)] = moves[lines - 1 :]
    return stays + carry_ref[pl.ds(7, lines)]


def advance_kernel(offsets, fractions, factors, up, main, down, out, grid, once, final, carry, twice, sems):
    rows, lines = final.shape[0], final.shape[1]
    blocks = main.shape[0]
    per = lines // blocks
    ext = rows + 4

    copies = [
        pltpu.make_async_copy(up, grid.at[pl.ds(0, HALO)], sems.at[0]),
        pltpu.make_async_copy(down, grid.at[pl.ds(HALO + rows, HALO)], sems.at[1]),
    ]
    for block in range(blocks):
        for c in range(per):
            copies.append(
                pltpu.make_async_copy(
                    main.at[block, :, pl.ds(c * LANES, LANES)],
                    grid.at[pl.ds(HALO, rows), block * per + c],
                    sems.at[2 + block * per + c],
                )
            )
    for copy in copies:
        copy.start()
    for copy in copies:
        copy.wait()

    def first_step(i, _):
        row = diffused(grid[i], grid[i + 1], grid[i + 2], grid[i + 3], grid[i + 4], factors[i])
        row = partly_shifted(row, offsets[0, i], fractions[0, i], carry.at[0])
        once[i, pl.ds(0, lines)] = row
        once[i, pl.ds(lines, lines)] = row
        return _

    lax.fori_loop(0, ext, first_step, 0)

    def moved(i):
        return once[i, pl.ds(lines - (offsets[0, i] >> 7), lines)]

    def second_step(i, _):
        row = diffused(moved(i), moved(i + 1), moved(i + 2), moved(i + 3), moved(i + 4), factors[i + 2])
        row = partly_shifted(row, offsets[1, i + 2], fractions[1, i + 2], carry.at[0])
        twice[0, pl.ds(0, lines)] = row
        twice[0, pl.ds(lines, lines)] = row
        final[i] = twice[0, pl.ds(lines - (offsets[1, i + 2] >> 7), lines)]
        return _

    lax.fori_loop(0, rows, second_step, 0)

    copies = []
    for block in range(blocks):
        for c in range(per):
            copies.append(
                pltpu.make_async_copy(
                    final.at[:, block * per + c],
                    out.at[block, :, pl.ds(c * LANES, LANES)],
                    sems.at[2 + block * per + c],
                )
            )
    for copy in copies:
        copy.start()
    for copy in copies:
        copy.wait()


def advance(offsets, fractions, factors, up, main, down):
    blocks, rows, width = main.shape
    lines = blocks * width // LANES
    smem = pl.BlockSpec(memory_space=pltpu.SMEM)
    anywhere = pl.BlockSpec(memory_space=pl.ANY)
    return pl.pallas_call(
        advance_kernel,
        out_shape=jax.ShapeDtypeStruct(main.shape, main.dtype),
        in_specs=[smem] * 3 + [anywhere] * 3,
        out_specs=anywhere,
        scratch_shapes=[
            pltpu.VMEM((rows + 2 * HALO, lines, LANES), jnp.float32),
            pltpu.VMEM((rows + 4, 2 * lines, LANES), jnp.float32),
            pltpu.VMEM((rows, lines, LANES), jnp.float32),
            pltpu.VMEM((1, lines + 8, LANES), jnp.float32),
            pltpu.VMEM((1, 2 * lines, LANES), jnp.float32),
            pltpu.SemaphoreType.DMA((2 + lines,)),
        ],
        compiler_params=pltpu.CompilerParams(vmem_limit_bytes=32 << 20),
    )(offsets, fractions, factors, up, main, down)


def from_neighbours(first, last, axis):
    peers = lax.axis_size(axis)
    forth = [(i, i + 1) for i in range(peers - 1)]
    back = [(j, i) for i, j in forth]
    return lax.ppermute(last, axis, forth), lax.ppermute(first, axis, back)


def as_rows(part):
    blocks, rows, width = part.shape
    cut = part.reshape(blocks, rows, width // LANES, LANES)
    return jnp.transpose(cut, (1, 0, 2, 3)).reshape(rows, blocks * width // LANES, LANES)


def shards(fields, offsets, fractions, coefs):
    shape = fields.shape
    rows, width = shape[2], shape[3]
    packed = jnp.concatenate([offsets.astype(jnp.float32), fractions, coefs[None] / 12.0])
    before, after = from_neighbours(packed[:, :2], packed[:, rows - 2 :], "rad")
    packed = jnp.concatenate([before, packed, after], axis=1)
    steps = offsets.shape[0]

    main = lax.all_to_all(fields.reshape(-1, rows, width), "azi", 0, 0, tiled=True)
    up, down = from_neighbours(as_rows(main[:, :HALO]), as_rows(main[:, rows - HALO :]), "rad")
    done = advance(
        packed[:steps].astype(jnp.int32), packed[steps : 2 * steps], packed[2 * steps], up, main, down
    )
    return lax.all_to_all(done, "azi", 0, 0, tiled=True).reshape(shape)


def solution(mesh):
    placed = (P(None, None, "rad", "azi"), P(None, "rad"), P(None, "rad"), P("rad"))
    return jax.shard_map(
        shards, mesh=mesh, in_specs=placed, out_specs=P(None, None, "rad", "azi"), check_vma=False
    )
```

```python
import jax
import jax.numpy as jnp
from jax import lax
from jax.experimental import pallas as pl
from jax.experimental.pallas import tpu as pltpu
from jax.sharding import PartitionSpec as P

LANES = 128
REACH = 2
HALO = 2 * REACH
TILE = 8


def diffused(far_up, up, here, down, far_down, factor):
    return here + factor * (16.0 * (up + down) - (far_up + far_down) - 30.0 * here)


def partly_shifted(row, shift, weight):
    part = shift & (LANES - 1)
    lane = lax.broadcasted_iota(jnp.int32, row[0].shape, 1)
    own_first, own_behind = lane >= part, lane > part
    first = [pltpu.roll(line, part, 1) for line in row]
    behind = [pltpu.roll(line, (part + 1) & (LANES - 1), 1) for line in row]
    first = [pltpu.roll(first[-1], 1, 0)] + first
    behind = [pltpu.roll(behind[-1], 1, 0)] + behind
    return [
        (1.0 - weight) * jnp.where(own_first, first[c + 1], first[c])
        + weight * jnp.where(own_behind, behind[c + 1], behind[c])
        for c in range(len(row))
    ]


def keep(ref, i, row):
    blocks = row[0].shape[0]
    for c, line in enumerate(row):
        ref[i, c, pl.ds(0, blocks)] = line
        ref[i, c, pl.ds(blocks, blocks)] = line


def moved(ref, i, shift):
    per, blocks = ref.shape[1], ref.shape[2] // 2
    lines = shift // LANES
    some, whole = lines % per, lines // per
    row = []
    for c in range(per):
        wraps = (c < some).astype(jnp.int32)
        row.append(ref[i, c - some + wraps * per, pl.ds(blocks - whole - wraps, blocks)])
    return row


def in_groups(count, size, body):
    size = next(s for s in range(size, 0, -1) if count % s == 0)

    def group(t, carry):
        body(t * size, size)
        return carry

    lax.fori_loop(0, count // size, group, 0)


def two_steps(offsets, fractions, factors, base, grid, once, twice, to):
    per = grid.shape[1]
    rows = grid.shape[0] - 2 * HALO

    def first_step(start, size):
        for u in range(size):
            i = start + u
            at = base + REACH + i
            row = [diffused(*[grid[i + j, c] for j in range(2 * REACH + 1)], factors[at]) for c in range(per)]
            keep(once, i, partly_shifted(row, offsets[0, at], fractions[0, at]))

    def second_step(start, size):
        lines = [moved(once, start + j, offsets[0, base + REACH + start + j]) for j in range(size + 2 * REACH)]
        for u in range(size):
            i = start + u
            at = base + HALO + i
            row = [diffused(*[lines[u + j][c] for j in range(2 * REACH + 1)], factors[at]) for c in range(per)]
            keep(twice, to + i, partly_shifted(row, offsets[1, at], fractions[1, at]))

    in_groups(rows + 2 * REACH, 4, first_step)
    in_groups(rows, 4, second_step)


def write(offsets, base, twice, start, count, out, to):
    def some(first, size):
        for u in range(size):
            i = first + u
            out[:, to + i, :] = jnp.concatenate(moved(twice, start + i, offsets[1, base + i]), axis=1)

    in_groups(count, 4, some)


def load(grid, at, source, row):
    line = source[:, row, :]
    for c in range(grid.shape[1]):
        grid[at, c] = line[:, c * LANES : (c + 1) * LANES]


def inner_kernel(offsets, fractions, factors, main, out, grid, once, twice, laid, sem):
    rows = main.shape[1]

    def relay(start, size):
        for u in range(size):
            load(grid, start + u, main, start + u)

    in_groups(rows, 4, relay)
    two_steps(offsets, fractions, factors, 0, grid, once, twice, 0)
    write(offsets, HALO, twice, 0, rows - 2 * HALO, laid, HALO)
    copy = pltpu.make_async_copy(laid, out, sem)
    copy.start()
    copy.wait()


def edge_kernel(offsets, fractions, factors, halo, main, given, out, grid, once, twice, laid, sems):
    rows = main.shape[1]
    inside = rows - 2 * HALO
    near = [pl.ds(0, TILE), pl.ds(rows - TILE, TILE)]
    fetches = [pltpu.make_async_copy(given.at[:, near[s]], laid.at[s], sems.at[s]) for s in range(2)]
    for fetch in fetches:
        fetch.start()
    stores = []
    for side in range(2):
        base = side * (inside + HALO)
        for r in range(HALO):
            load(grid, r + side * 2 * HALO, halo, side * HALO + r)
        for r in range(2 * HALO):
            load(grid, r + (1 - side) * HALO, main, r + side * inside)
        two_steps(offsets, fractions, factors, base, grid, once, twice, side * HALO)
        fetches[side].wait()
        write(offsets, base + HALO, twice, side * HALO, HALO, laid.at[side], side * (TILE - HALO))
        stores.append(pltpu.make_async_copy(laid.at[side], out.at[:, near[side]], sems.at[side]))
        stores[-1].start()
    for store in stores:
        store.wait()


def call(kernel, tables, arrays, kept, out, scratch, sems, vmem):
    smem = pl.BlockSpec(memory_space=pltpu.SMEM)
    local = pl.BlockSpec(memory_space=pltpu.VMEM)
    far = pl.BlockSpec(memory_space=pltpu.HBM)
    given = len(tables) + len(arrays)
    return pl.pallas_call(
        kernel,
        out_shape=pltpu.HBM(out, jnp.float32),
        in_specs=[smem] * len(tables) + [local] * len(arrays) + [far] * len(kept),
        out_specs=far,
        scratch_shapes=[pltpu.VMEM(shape, jnp.float32) for shape in scratch] + [sems],
        input_output_aliases={given + i: i for i in range(len(kept))},
        compiler_params=pltpu.CompilerParams(vmem_limit_bytes=vmem << 20),
    )(*tables, *arrays, *[pltpu.with_memory_space_constraint(k, pltpu.HBM) for k in kept])


def from_neighbours(first, last, axis):
    peers = lax.axis_size(axis)
    forth = [(i, i + 1) for i in range(peers - 1)]
    back = [(j, i) for i, j in forth]
    return lax.ppermute(last, axis, forth), lax.ppermute(first, axis, back)


def shards(fields, offsets, fractions, coefs):
    shape = fields.shape
    rows, width = shape[2], shape[3]
    steps = offsets.shape[0]
    blocks = fields.reshape(-1, rows, width)
    factors = coefs / 12.0

    main = lax.all_to_all(blocks, "azi", 0, 0, tiled=True)

    packed = jnp.concatenate([offsets.astype(jnp.float32), fractions, factors[None]])
    before, after = from_neighbours(packed[:, :HALO], packed[:, rows - HALO :], "rad")
    packed = jnp.concatenate([before, packed, after], axis=1)
    halo = jnp.concatenate(from_neighbours(blocks[:, :HALO], blocks[:, rows - HALO :], "rad"), axis=1)
    halo = lax.all_to_all(halo, "azi", 0, 0, tiled=True)

    members, per = blocks.shape[0], width // LANES

    def single(count):
        return (count, per, members, LANES)

    def double(count):
        return (count, per, 2 * members, LANES)

    inside = rows - 2 * HALO
    done = call(
        inner_kernel,
        (offsets, fractions, factors),
        (main,),
        (),
        main.shape,
        [single(rows), double(rows - 2 * REACH), double(inside), main.shape],
        pltpu.SemaphoreType.DMA,
        16,
    )
    tables = (packed[:steps].astype(jnp.int32), packed[steps : 2 * steps], packed[2 * steps])
    done = call(
        edge_kernel,
        tables,
        (halo, main),
        (done,),
        main.shape,
        [single(3 * HALO), double(HALO + 2 * REACH), double(2 * HALO), (2, members, TILE, width)],
        pltpu.SemaphoreType.DMA((2,)),
        4,
    )
    return lax.all_to_all(done, "azi", 0, 0, tiled=True).reshape(shape)


def solution(mesh):
    placed = (P(None, None, "rad", "azi"), P(None, "rad"), P(None, "rad"), P("rad"))
    return jax.shard_map(
        shards, mesh=mesh, in_specs=placed, out_specs=P(None, None, "rad", "azi"), check_vma=False
    )
```

```python
import jax
import jax.numpy as jnp
from jax import lax
from jax.experimental import pallas as pl
from jax.experimental.pallas import tpu as pltpu
from jax.sharding import PartitionSpec as P

LANES = 128
REACH = 2
HALO = 2 * REACH


def diffused(far_up, up, here, down, far_down, factor):
    return here + factor * (16.0 * (up + down) - (far_up + far_down) - 30.0 * here)


def partly_shifted(row, shift, weight):
    part = shift & (LANES - 1)
    lane = lax.broadcasted_iota(jnp.int32, row[0].shape, 1)
    own_first, own_behind = lane >= part, lane > part
    first = [pltpu.roll(line, part, 1) for line in row]
    behind = [pltpu.roll(line, (part + 1) & (LANES - 1), 1) for line in row]
    first = [pltpu.roll(first[-1], 1, 0)] + first
    behind = [pltpu.roll(behind[-1], 1, 0)] + behind
    return [
        (1.0 - weight) * jnp.where(own_first, first[c + 1], first[c])
        + weight * jnp.where(own_behind, behind[c + 1], behind[c])
        for c in range(len(row))
    ]


def keep(ref, i, row):
    blocks = row[0].shape[0]
    for c, line in enumerate(row):
        ref[i, c, pl.ds(0, blocks)] = line
        ref[i, c, pl.ds(blocks, blocks)] = line


def moved(ref, i, shift):
    per, blocks = ref.shape[1], ref.shape[2] // 2
    lines = shift // LANES
    some, whole = lines % per, lines // per
    row = []
    for c in range(per):
        wraps = (c < some).astype(jnp.int32)
        row.append(ref[i, c - some + wraps * per, pl.ds(blocks - whole - wraps, blocks)])
    return row


def in_groups(count, size, body):
    size = next(s for s in range(size, 0, -1) if count % s == 0)

    def group(t, carry):
        body(t * size, size)
        return carry

    lax.fori_loop(0, count // size, group, 0)


def advance_kernel(offsets, fractions, factors, main, out, grid, once, twice):
    rows, per = out.shape[1], grid.shape[1]

    def relay(at, row):
        line = main[:, row, :]
        for c in range(per):
            grid[at, c] = line[:, c * LANES : (c + 1) * LANES]

    def relay_group(start, size):
        for u in range(size):
            relay(HALO + start + u, start + u)

    def first_step(start, size):
        for u in range(size):
            i = start + u
            at = REACH + i
            row = [diffused(*[grid[i + j, c] for j in range(2 * REACH + 1)], factors[at]) for c in range(per)]
            keep(once, i, partly_shifted(row, offsets[0, at], fractions[0, at]))

    def second_step(start, size):
        lines = [moved(once, start + j, offsets[0, REACH + start + j]) for j in range(size + 2 * REACH)]
        for u in range(size):
            i = start + u
            at = HALO + i
            row = [diffused(*[lines[u + j][c] for j in range(2 * REACH + 1)], factors[at]) for c in range(per)]
            keep(twice, i, partly_shifted(row, offsets[1, at], fractions[1, at]))

    def write(start, size):
        for u in range(size):
            i = start + u
            out[:, i, :] = jnp.concatenate(moved(twice, i, offsets[1, HALO + i]), axis=1)

    for r in range(HALO):
        relay(r, rows + r)
        relay(HALO + rows + r, rows + HALO + r)
    in_groups(rows, 4, relay_group)
    in_groups(rows + 2 * REACH, 4, first_step)
    in_groups(rows, 4, second_step)
    in_groups(rows, 4, write)


def advance(offsets, fractions, factors, main):
    members, extended, width = main.shape
    rows, per = extended - 2 * HALO, width // LANES
    smem = pl.BlockSpec(memory_space=pltpu.SMEM)
    vmem = pl.BlockSpec(memory_space=pltpu.VMEM)
    return pl.pallas_call(
        advance_kernel,
        out_shape=jax.ShapeDtypeStruct((members, rows, width), jnp.float32),
        in_specs=[smem] * 3 + [vmem],
        out_specs=vmem,
        scratch_shapes=[
            pltpu.VMEM((extended, per, members, LANES), jnp.float32),
            pltpu.VMEM((rows + 2 * REACH, per, 2 * members, LANES), jnp.float32),
            pltpu.VMEM((rows, per, 2 * members, LANES), jnp.float32),
        ],
        compiler_params=pltpu.CompilerParams(vmem_limit_bytes=16 << 20),
    )(offsets, fractions, factors, main)


def from_neighbours(first, last, axis):
    peers = lax.axis_size(axis)
    forth = [(i, i + 1) for i in range(peers - 1)]
    back = [(j, i) for i, j in forth]
    return lax.ppermute(last, axis, forth), lax.ppermute(first, axis, back)


def shards(fields, offsets, fractions, coefs):
    shape = fields.shape
    rows, width = shape[2], shape[3]
    steps = offsets.shape[0]
    blocks = fields.reshape(-1, rows, width)
    before, after = from_neighbours(blocks[:, :HALO], blocks[:, rows - HALO :], "rad")
    main = jnp.concatenate([blocks, before, after], axis=1)

    table = jnp.concatenate([offsets.astype(jnp.float32), fractions, coefs[None] / 12.0])
    table = lax.all_gather(table, "rad", axis=1, tiled=True)
    table = jnp.pad(table, ((0, 0), (HALO, HALO)))
    table = lax.dynamic_slice_in_dim(table, lax.axis_index("rad") * rows, rows + 2 * HALO, axis=1)

    main = lax.all_to_all(main, "azi", 0, 0, tiled=True)
    done = advance(table[:steps].astype(jnp.int32), table[steps : 2 * steps], table[2 * steps], main)
    return lax.all_to_all(done, "azi", 0, 0, tiled=True).reshape(shape)


def solution(mesh):
    placed = (P(None, None, "rad", "azi"), P(None, "rad"), P(None, "rad"), P("rad"))
    return jax.shard_map(
        shards, mesh=mesh, in_specs=placed, out_specs=P(None, None, "rad", "azi"), check_vma=False
    )
```

```python
import jax
import jax.numpy as jnp
from jax import lax
from jax.experimental import pallas as pl
from jax.experimental.pallas import tpu as pltpu
from jax.sharding import PartitionSpec as P

LANES = 128
REACH = 2
HALO = 2 * REACH
TILE = 8


def diffused(far_up, up, here, down, far_down, factor):
    return here + factor * (16.0 * (up + down) - (far_up + far_down) - 30.0 * here)


def partly_shifted(row, shift, weight):
    part = shift & (LANES - 1)
    lane = lax.broadcasted_iota(jnp.int32, row[0].shape, 1)
    own_first, own_behind = lane >= part, lane > part
    first = [pltpu.roll(line, part, 1) for line in row]
    behind = [pltpu.roll(line, (part + 1) & (LANES - 1), 1) for line in row]
    first = [pltpu.roll(first[-1], 1, 0)] + first
    behind = [pltpu.roll(behind[-1], 1, 0)] + behind
    return [
        (1.0 - weight) * jnp.where(own_first, first[c + 1], first[c])
        + weight * jnp.where(own_behind, behind[c + 1], behind[c])
        for c in range(len(row))
    ]


def keep(ref, i, row):
    blocks = row[0].shape[0]
    for c, line in enumerate(row):
        ref[i, c, pl.ds(0, blocks)] = line
        ref[i, c, pl.ds(blocks, blocks)] = line


def moved(ref, i, shift):
    per, blocks = ref.shape[1], ref.shape[2] // 2
    lines = shift >> 7
    some, whole = lines & (per - 1), lines >> (per.bit_length() - 1)
    row = []
    for c in range(per):
        wraps = (c < some).astype(jnp.int32)
        row.append(ref[i, c - some + wraps * per, pl.ds(blocks - whole - wraps, blocks)])
    return row


def in_groups(count, size, body):
    size = next(s for s in range(size, 0, -1) if count % s == 0)

    def group(t, carry):
        body(t * size, size)
        return carry

    lax.fori_loop(0, count // size, group, 0)


def two_steps(offsets, fractions, factors, base, grid, once, twice, to):
    per = grid.shape[1]
    rows = grid.shape[0] - 2 * HALO

    def first_step(start, size):
        for u in range(size):
            i = start + u
            at = base + REACH + i
            row = [diffused(*[grid[i + j, c] for j in range(2 * REACH + 1)], factors[at]) for c in range(per)]
            keep(once, i, partly_shifted(row, offsets[0, at], fractions[0, at]))

    def second_step(start, size):
        lines = [moved(once, start + j, offsets[0, base + REACH + start + j]) for j in range(size + 2 * REACH)]
        for u in range(size):
            i = start + u
            at = base + HALO + i
            row = [diffused(*[lines[u + j][c] for j in range(2 * REACH + 1)], factors[at]) for c in range(per)]
            keep(twice, to + i, partly_shifted(row, offsets[1, at], fractions[1, at]))

    in_groups(rows + 2 * REACH, 4, first_step)
    in_groups(rows, 4, second_step)


def write(offsets, base, twice, start, count, out, to):
    def some(first, size):
        for u in range(size):
            i = first + u
            out[:, to + i, :] = jnp.concatenate(moved(twice, start + i, offsets[1, base + i]), axis=1)

    in_groups(count, 4, some)


def load(grid, at, source, row):
    line = source[:, row, :]
    for c in range(grid.shape[1]):
        grid[at, c] = line[:, c * LANES : (c + 1) * LANES]


def inner_kernel(offsets, fractions, factors, main, out, grid, once, twice, laid, sems):
    rows = main.shape[1]

    def relay(start, size):
        for u in range(size):
            load(grid, start + u, main, start + u)

    in_groups(rows, 4, relay)
    two_steps(offsets, fractions, factors, 0, grid, once, twice, 0)
    copies = []
    for tile in range(rows // TILE):
        lo, hi = max(tile * TILE, HALO), min((tile + 1) * TILE, rows - HALO)
        write(offsets, lo, twice, lo - HALO, hi - lo, laid, lo)
        here = pl.ds(tile * TILE, TILE)
        copies.append(pltpu.make_async_copy(laid.at[:, here], out.at[:, here], sems.at[tile]))
        copies[-1].start()
    for copy in copies:
        copy.wait()


def edge_kernel(offsets, fractions, factors, before, after, main, given, out, grid, once, twice, laid, sems):
    rows = main.shape[1]
    inside = rows - 2 * HALO
    near = [pl.ds(0, TILE), pl.ds(rows - TILE, TILE)]
    fetches = [pltpu.make_async_copy(given.at[:, near[s]], laid.at[s], sems.at[s]) for s in range(2)]
    for fetch in fetches:
        fetch.start()
    stores = []
    for side in range(2):
        base = side * (inside + HALO)
        for r in range(HALO):
            load(grid, r + side * 2 * HALO, (before, after)[side], r)
        for r in range(2 * HALO):
            load(grid, r + (1 - side) * HALO, main, r + side * inside)
        two_steps(offsets, fractions, factors, base, grid, once, twice, side * HALO)
        fetches[side].wait()
        write(offsets, base + HALO, twice, side * HALO, HALO, laid.at[side], side * (TILE - HALO))
        stores.append(pltpu.make_async_copy(laid.at[side], out.at[:, near[side]], sems.at[side]))
        stores[-1].start()
    for store in stores:
        store.wait()


def call(kernel, tables, arrays, kept, out, scratch, sems, vmem):
    smem = pl.BlockSpec(memory_space=pltpu.SMEM)
    local = pl.BlockSpec(memory_space=pltpu.VMEM)
    far = pl.BlockSpec(memory_space=pltpu.HBM)
    given = len(tables) + len(arrays)
    return pl.pallas_call(
        kernel,
        out_shape=pltpu.HBM(out, jnp.float32),
        in_specs=[smem] * len(tables) + [local] * len(arrays) + [far] * len(kept),
        out_specs=far,
        scratch_shapes=[pltpu.VMEM(shape, jnp.float32) for shape in scratch] + [sems],
        input_output_aliases={given + i: i for i in range(len(kept))},
        compiler_params=pltpu.CompilerParams(vmem_limit_bytes=vmem << 20),
    )(*tables, *arrays, *[pltpu.with_memory_space_constraint(k, pltpu.HBM) for k in kept])


def from_neighbours(first, last, axis):
    peers = lax.axis_size(axis)
    forth = [(i, i + 1) for i in range(peers - 1)]
    back = [(j, i) for i, j in forth]
    return lax.ppermute(last, axis, forth), lax.ppermute(first, axis, back)


def shards(fields, offsets, fractions, coefs):
    shape = fields.shape
    rows, width = shape[2], shape[3]
    steps = offsets.shape[0]
    blocks = fields.reshape(-1, rows, width)
    factors = coefs / 12.0

    main = lax.all_to_all(blocks, "azi", 0, 0, tiled=True)
    halo = from_neighbours(main[:, :HALO], main[:, rows - HALO :], "rad")

    table = jnp.concatenate([offsets.astype(jnp.float32), fractions, factors[None]])
    before, after = from_neighbours(table[:, :HALO], table[:, rows - HALO :], "rad")
    table = jnp.concatenate([before, table, after], axis=1)

    members, per = blocks.shape[0], width // LANES

    def single(count):
        return (count, per, members, LANES)

    def double(count):
        return (count, per, 2 * members, LANES)

    inside = rows - 2 * HALO
    done = call(
        inner_kernel,
        (offsets, fractions, factors),
        (main,),
        (),
        main.shape,
        [single(rows), double(rows - 2 * REACH), double(inside), main.shape],
        pltpu.SemaphoreType.DMA((rows // TILE,)),
        16,
    )
    tables = (table[:steps].astype(jnp.int32), table[steps : 2 * steps], table[2 * steps])
    done = call(
        edge_kernel,
        tables,
        (*halo, main),
        (done,),
        main.shape,
        [single(3 * HALO), double(HALO + 2 * REACH), double(2 * HALO), (2, members, TILE, width)],
        pltpu.SemaphoreType.DMA((2,)),
        4,
    )
    return lax.all_to_all(done, "azi", 0, 0, tiled=True).reshape(shape)


def solution(mesh):
    placed = (P(None, None, "rad", "azi"), P(None, "rad"), P(None, "rad"), P("rad"))
    return jax.shard_map(
        shards, mesh=mesh, in_specs=placed, out_specs=P(None, None, "rad", "azi"), check_vma=False
    )
```

```python
import jax
import jax.numpy as jnp
from jax import lax
from jax.experimental import pallas as pl
from jax.experimental.pallas import tpu as pltpu
from jax.sharding import PartitionSpec as P

LANES = 128
TILE = 8
REACH = 2
HALO = 2 * REACH


def diffused(far_up, up, here, down, far_down, factor):
    return here + factor * (16.0 * (up + down) - (far_up + far_down) - 30.0 * here)


def partly_shifted(row, shift, weight):
    part = shift & (LANES - 1)
    lane = lax.broadcasted_iota(jnp.int32, row[0].shape, 1)
    own_first, own_behind = lane >= part, lane > part
    first = [pltpu.roll(line, part, 1) for line in row]
    behind = [pltpu.roll(line, (part + 1) & (LANES - 1), 1) for line in row]
    first = [pltpu.roll(first[-1], 1, 0)] + first
    behind = [pltpu.roll(behind[-1], 1, 0)] + behind
    return [
        (1.0 - weight) * jnp.where(own_first, first[c + 1], first[c])
        + weight * jnp.where(own_behind, behind[c + 1], behind[c])
        for c in range(len(row))
    ]


def keep(ref, i, row):
    blocks = row[0].shape[0]
    for c, line in enumerate(row):
        ref[i, c, pl.ds(0, blocks)] = line
        ref[i, c, pl.ds(blocks, blocks)] = line


def moved(ref, i, shift):
    per, blocks = ref.shape[1], ref.shape[2] // 2
    lines = shift >> 7
    some, whole = lines & (per - 1), lines >> (per.bit_length() - 1)
    row = []
    for c in range(per):
        wraps = (c < some).astype(jnp.int32)
        row.append(ref[i, c - some + wraps * per, pl.ds(blocks - whole - wraps, blocks)])
    return row


def in_groups(count, size, body):
    size = next(s for s in range(size, 0, -1) if count % s == 0)

    def group(t, carry):
        body(t * size, size)
        return carry

    lax.fori_loop(0, count // size, group, 0)


def at_once(count, size, body):
    body(0, count)


def two_steps(loop, offset, fraction, factor, grid, once, twice):
    per = grid.shape[1]
    rows = grid.shape[0] - 2 * HALO

    def first_step(start, size):
        for u in range(size):
            i = start + u
            at = i + REACH
            row = [diffused(*[grid[i + j, c] for j in range(2 * REACH + 1)], factor(at)) for c in range(per)]
            keep(once, i, partly_shifted(row, offset(0, at), fraction(0, at)))

    def second_step(start, size):
        lines = [moved(once, start + j, offset(0, start + j + REACH)) for j in range(size + 2 * REACH)]
        for u in range(size):
            i = start + u
            at = i + HALO
            row = [diffused(*[lines[u + j][c] for j in range(2 * REACH + 1)], factor(at)) for c in range(per)]
            keep(twice, i, partly_shifted(row, offset(1, at), fraction(1, at)))

    loop(rows + 2 * REACH, 4, first_step)
    loop(rows, 4, second_step)


def write(loop, offset, twice, start, count, out, to):
    def some(first, size):
        for u in range(size):
            i = first + u
            out[:, to + i, :] = jnp.concatenate(moved(twice, start + i, offset(start + i)), axis=1)

    loop(count, 4, some)


def load(grid, at, source, row):
    line = source[pl.ds(0, grid.shape[2]), row, :]
    for c in range(grid.shape[1]):
        grid[at, c] = line[:, c * LANES : (c + 1) * LANES]


def edge_radii_kernel(main, table, first, last):
    members, rows, _ = main.shape
    first[pl.ds(0, members)] = main[:, :HALO]
    first[members] = table[0]
    last[pl.ds(0, members)] = main[:, rows - HALO :]
    last[members] = table[1]


def inner_kernel(offsets, fractions, factors, main, out, grid, once, twice, laid, sems):
    rows = main.shape[1]

    def relay(start, size):
        for u in range(size):
            load(grid, start + u, main, start + u)

    in_groups(rows, 4, relay)
    two_steps(
        in_groups,
        lambda step, at: offsets[step, at],
        lambda step, at: fractions[step, at],
        lambda at: factors[at],
        grid,
        once,
        twice,
    )
    copies = []
    for tile in range(rows // TILE):
        lo, hi = max(tile * TILE, HALO), min((tile + 1) * TILE, rows - HALO)
        write(in_groups, lambda i: offsets[1, i + HALO], twice, lo - HALO, hi - lo, laid, lo)
        here = pl.ds(tile * TILE, TILE)
        copies.append(pltpu.make_async_copy(laid.at[:, here], out.at[:, here], sems.at[tile]))
        copies[-1].start()
    for copy in copies:
        copy.wait()


def edge_kernel(offsets, fractions, factors, before, after, main, given, out, grid, once, twice, laid, table, sems):
    members, rows, _ = main.shape
    steps = offsets.shape[0]
    near = [pl.ds(0, TILE), pl.ds(rows - TILE, TILE)]
    tables = [
        pltpu.make_async_copy(halo.at[members, :, pl.ds(0, LANES)], table.at[side], sems.at[side])
        for side, halo in enumerate((before, after))
    ]
    fetches = [pltpu.make_async_copy(given.at[:, near[side]], laid.at[side], sems.at[2 + side]) for side in range(2)]
    for copy in tables + fetches:
        copy.start()

    for side, halo in enumerate((before, after)):
        for r in range(HALO):
            load(grid.at[side], r + side * 2 * HALO, halo, r)
        for r in range(2 * HALO):
            load(grid.at[side], r + (1 - side) * HALO, main, r + side * (rows - 2 * HALO))
    for copy in tables:
        copy.wait()

    stores = []
    for side in range(2):

        def entry(own, column, at, side=side):
            own_row = at - HALO if side == 0 else at + rows - 2 * HALO
            if 0 <= own_row < rows:
                return own(own_row)
            return table[side, own_row + HALO if side == 0 else own_row - rows, column]

        def offset(step, at, entry=entry):
            return entry(lambda r: offsets[step, r], step, at)

        def fraction(step, at, entry=entry):
            return entry(lambda r: fractions[step, r], steps + step, at)

        def factor(at, entry=entry):
            return entry(lambda r: factors[r], 2 * steps, at)

        def whole(step, at, offset=offset):
            return offset(step, at).astype(jnp.int32)

        two_steps(at_once, whole, fraction, factor, grid.at[side], once.at[side], twice.at[side])
        fetches[side].wait()
        write(
            at_once,
            lambda i, whole=whole: whole(1, i + HALO),
            twice.at[side],
            0,
            HALO,
            laid.at[side],
            side * (TILE - HALO),
        )
        stores.append(pltpu.make_async_copy(laid.at[side], out.at[:, near[side]], sems.at[2 + side]))
        stores[-1].start()
    for store in stores:
        store.wait()


SMEM = pl.BlockSpec(memory_space=pltpu.SMEM)
VMEM = pl.BlockSpec(memory_space=pltpu.VMEM)
FAR = pl.BlockSpec(memory_space=pltpu.HBM)


def grant(mebibytes):
    return pltpu.CompilerParams(vmem_limit_bytes=mebibytes << 20)


def edge_radii(main, table):
    members, _, width = main.shape
    side = jax.ShapeDtypeStruct((members + 1, HALO, width), jnp.float32)
    return pl.pallas_call(
        edge_radii_kernel,
        out_shape=[side, side],
        in_specs=[VMEM, VMEM],
        out_specs=[VMEM, VMEM],
        compiler_params=grant(2),
    )(main, table)


def inner(offsets, fractions, factors, main):
    members, rows, width = main.shape
    per = width // LANES
    return pl.pallas_call(
        inner_kernel,
        out_shape=pltpu.HBM(main.shape, jnp.float32),
        in_specs=[SMEM] * 3 + [VMEM],
        out_specs=FAR,
        scratch_shapes=[
            pltpu.VMEM((rows, per, members, LANES), jnp.float32),
            pltpu.VMEM((rows - 2 * REACH, per, 2 * members, LANES), jnp.float32),
            pltpu.VMEM((rows - 2 * HALO, per, 2 * members, LANES), jnp.float32),
            pltpu.VMEM(main.shape, jnp.float32),
            pltpu.SemaphoreType.DMA((rows // TILE,)),
        ],
        compiler_params=grant(16),
    )(offsets, fractions, factors, main)


def edges(offsets, fractions, factors, before, after, main, done):
    members, _, width = main.shape
    per = width // LANES
    return pl.pallas_call(
        edge_kernel,
        out_shape=pltpu.HBM(main.shape, jnp.float32),
        in_specs=[SMEM] * 3 + [VMEM] * 3 + [FAR],
        out_specs=FAR,
        scratch_shapes=[
            pltpu.VMEM((2, 3 * HALO, per, members, LANES), jnp.float32),
            pltpu.VMEM((2, HALO + 2 * REACH, per, 2 * members, LANES), jnp.float32),
            pltpu.VMEM((2, HALO, per, 2 * members, LANES), jnp.float32),
            pltpu.VMEM((2, members, TILE, width), jnp.float32),
            pltpu.SMEM((2, HALO, LANES), jnp.float32),
            pltpu.SemaphoreType.DMA((4,)),
        ],
        input_output_aliases={6: 0},
        compiler_params=grant(6),
    )(offsets, fractions, factors, before, after, main, pltpu.with_memory_space_constraint(done, pltpu.HBM))


def from_neighbours(first, last, axis):
    peers = lax.axis_size(axis)
    forth = [(i, i + 1) for i in range(peers - 1)]
    back = [(j, i) for i, j in forth]
    return lax.ppermute(last, axis, forth), lax.ppermute(first, axis, back)


def shards(fields, offsets, fractions, coefs):
    shape = fields.shape
    rows, width = shape[2], shape[3]
    blocks = fields.reshape(-1, rows, width)
    factors = coefs / 12.0
    main = lax.all_to_all(blocks, "azi", 0, 0, tiled=True)

    table = jnp.concatenate([offsets.astype(jnp.float32), fractions, factors[None]]).T
    table = jnp.stack([table[:HALO], table[rows - HALO :]])
    table = jnp.pad(table, ((0, 0), (0, 0), (0, width - table.shape[2])))

    before, after = from_neighbours(*edge_radii(main, table), "rad")
    done = inner(offsets, fractions, factors, main)
    done = edges(offsets, fractions, factors, before, after, main, done)
    return lax.all_to_all(done, "azi", 0, 0, tiled=True).reshape(shape)


def solution(mesh):
    placed = (P(None, None, "rad", "azi"), P(None, "rad"), P(None, "rad"), P("rad"))
    return jax.shard_map(
        shards, mesh=mesh, in_specs=placed, out_specs=P(None, None, "rad", "azi"), check_vma=False
    )
```

```python
import jax
import jax.numpy as jnp
from jax import lax
from jax.experimental import pallas as pl
from jax.experimental.pallas import tpu as pltpu
from jax.sharding import PartitionSpec as P

LANES = 128
TILE = 8
REACH = 2
HALO = 2 * REACH
RELAY, FIRST = 16, 60


def diffused(far_up, up, here, down, far_down, factor):
    return here + factor * (16.0 * (up + down) - (far_up + far_down) - 30.0 * here)


def partly_shifted(row, shift, weight):
    part = shift & (LANES - 1)
    lane = lax.broadcasted_iota(jnp.int32, row[0].shape, 1)
    own_first, own_behind = lane >= part, lane > part
    first = [pltpu.roll(line, part, 1) for line in row]
    behind = [pltpu.roll(line, (part + 1) & (LANES - 1), 1) for line in row]
    first = [pltpu.roll(first[-1], 1, 0)] + first
    behind = [pltpu.roll(behind[-1], 1, 0)] + behind
    return [
        (1.0 - weight) * jnp.where(own_first, first[c + 1], first[c])
        + weight * jnp.where(own_behind, behind[c + 1], behind[c])
        for c in range(len(row))
    ]


def keep(ref, i, row):
    blocks = row[0].shape[0]
    for c, line in enumerate(row):
        ref[i, c, pl.ds(0, blocks)] = line
        ref[i, c, pl.ds(blocks, blocks)] = line


def moved_line(ref, i, shift, c):
    per, blocks = ref.shape[1], ref.shape[2] // 2
    lines = shift >> 7
    some, whole = lines & (per - 1), lines >> (per.bit_length() - 1)
    wraps = (c < some).astype(jnp.int32)
    return ref[i, c - some + wraps * per, pl.ds(blocks - whole - wraps, blocks)]


def moved(ref, i, shift):
    return [moved_line(ref, i, shift, c) for c in range(ref.shape[1])]


def in_groups(count, size, body):
    size = next(s for s in range(size, 0, -1) if count % s == 0)

    def group(t, carry):
        body(t * size, size)
        return carry

    lax.fori_loop(0, count // size, group, 0)


def two_steps(offset, fraction, factor, grid, once, twice):
    per = grid.shape[1]

    def diffuse(start, size, at, number, line, out):
        rows = [[] for _ in range(size)]
        for c in range(per):
            read = [line(start + j, c) for j in range(size + 2 * REACH)]
            for u in range(size):
                rows[u].append(diffused(*read[u : u + 2 * REACH + 1], factor(start + u + at)))
        for u in range(size):
            here = start + u + at
            keep(out, start + u, partly_shifted(rows[u], offset(number, here), fraction(number, here)))

    def first_step(start, size):
        diffuse(start, size, REACH, 0, lambda i, c: grid[i, c], once)

    def second_step(start, size):
        diffuse(start, size, HALO, 1, lambda i, c: moved_line(once, i, offset(0, i + REACH), c), twice)

    return first_step, second_step


def write(offset, twice, start, count, out, to):
    for i in range(count):
        out[:, to + i, :] = jnp.concatenate(moved(twice, start + i, offset(start + i)), axis=1)


def load(grid, at, source, row):
    line = source[pl.ds(0, grid.shape[2]), row, :]
    for c in range(grid.shape[1]):
        grid[at, c] = line[:, c * LANES : (c + 1) * LANES]


def edge_radii_kernel(main, table, first, last):
    members, rows, _ = main.shape
    first[pl.ds(0, members)] = main[:, :HALO]
    first[members] = table[0]
    last[pl.ds(0, members)] = main[:, rows - HALO :]
    last[members] = table[1]


def inner_kernel(offsets, fractions, factors, main, out, grid, once, twice, laid, sems):
    rows = main.shape[1]

    def relay(start, size):
        for u in range(size):
            load(grid, start + u, main, start + u)

    first_step, second_step = two_steps(
        lambda step, at: offsets[step, at],
        lambda step, at: fractions[step, at],
        lambda at: factors[at],
        grid,
        once,
        twice,
    )
    in_groups(rows, RELAY, relay)
    in_groups(rows - 2 * REACH, FIRST, first_step)
    copies = []
    for tile in range(rows // TILE):
        lo, hi = max(tile * TILE, HALO), min((tile + 1) * TILE, rows - HALO)
        second_step(lo - HALO, hi - lo)
        write(lambda i: offsets[1, i + HALO], twice, lo - HALO, hi - lo, laid, lo)
        here = pl.ds(tile * TILE, TILE)
        copies.append(pltpu.make_async_copy(laid.at[:, here], out.at[:, here], sems.at[tile]))
        copies[-1].start()
    for copy in copies:
        copy.wait()


def edge_kernel(offsets, fractions, factors, before, after, main, given, out, grid, once, twice, laid, table, sems):
    members, rows, _ = main.shape
    steps = offsets.shape[0]
    near = [pl.ds(0, TILE), pl.ds(rows - TILE, TILE)]
    tables = [
        pltpu.make_async_copy(halo.at[members, :, pl.ds(0, LANES)], table.at[side], sems.at[side])
        for side, halo in enumerate((before, after))
    ]
    fetches = [pltpu.make_async_copy(given.at[:, near[side]], laid.at[side], sems.at[2 + side]) for side in range(2)]
    for copy in tables + fetches:
        copy.start()

    for side, halo in enumerate((before, after)):
        for r in range(HALO):
            load(grid.at[side], r + side * 2 * HALO, halo, r)
        for r in range(2 * HALO):
            load(grid.at[side], r + (1 - side) * HALO, main, r + side * (rows - 2 * HALO))
    for copy in tables:
        copy.wait()

    def side_steps(side):
        def entry(own, column, at):
            row = at - HALO if side == 0 else at + rows - 2 * HALO
            if 0 <= row < rows:
                return own(row)
            return table[side, row + HALO if side == 0 else row - rows, column]

        def offset(step, at):
            return entry(lambda row: offsets[step, row], step, at).astype(jnp.int32)

        def fraction(step, at):
            return entry(lambda row: fractions[step, row], steps + step, at)

        def factor(at):
            return entry(lambda row: factors[row], 2 * steps, at)

        first_step, second_step = two_steps(offset, fraction, factor, grid.at[side], once.at[side], twice.at[side])
        return offset, first_step, second_step

    sides = [side_steps(side) for side in range(2)]
    for _, first_step, _ in sides:
        first_step(0, HALO + 2 * REACH)
    for _, _, second_step in sides:
        second_step(0, HALO)
    for fetch in fetches:
        fetch.wait()
    stores = []
    for side, (offset, _, _) in enumerate(sides):
        write(lambda i, offset=offset: offset(1, i + HALO), twice.at[side], 0, HALO, laid.at[side], side * (TILE - HALO))
        stores.append(pltpu.make_async_copy(laid.at[side], out.at[:, near[side]], sems.at[2 + side]))
        stores[-1].start()
    for store in stores:
        store.wait()


SMEM = pl.BlockSpec(memory_space=pltpu.SMEM)
VMEM = pl.BlockSpec(memory_space=pltpu.VMEM)
FAR = pl.BlockSpec(memory_space=pltpu.HBM)


def grant(mebibytes):
    return pltpu.CompilerParams(vmem_limit_bytes=mebibytes << 20)


def edge_radii(main, table):
    members, _, width = main.shape
    side = jax.ShapeDtypeStruct((members + 1, HALO, width), jnp.float32)
    return pl.pallas_call(
        edge_radii_kernel,
        out_shape=[side, side],
        in_specs=[VMEM, VMEM],
        out_specs=[VMEM, VMEM],
        compiler_params=grant(2),
    )(main, table)


def inner(offsets, fractions, factors, main):
    members, rows, width = main.shape
    per = width // LANES
    return pl.pallas_call(
        inner_kernel,
        out_shape=pltpu.HBM(main.shape, jnp.float32),
        in_specs=[SMEM] * 3 + [VMEM],
        out_specs=FAR,
        scratch_shapes=[
            pltpu.VMEM((rows, per, members, LANES), jnp.float32),
            pltpu.VMEM((rows - 2 * REACH, per, 2 * members, LANES), jnp.float32),
            pltpu.VMEM((rows - 2 * HALO, per, 2 * members, LANES), jnp.float32),
            pltpu.VMEM(main.shape, jnp.float32),
            pltpu.SemaphoreType.DMA((rows // TILE,)),
        ],
        compiler_params=grant(16),
    )(offsets, fractions, factors, main)


def edges(offsets, fractions, factors, before, after, main, done):
    members, _, width = main.shape
    per = width // LANES
    return pl.pallas_call(
        edge_kernel,
        out_shape=pltpu.HBM(main.shape, jnp.float32),
        in_specs=[SMEM] * 3 + [VMEM] * 3 + [FAR],
        out_specs=FAR,
        scratch_shapes=[
            pltpu.VMEM((2, 3 * HALO, per, members, LANES), jnp.float32),
            pltpu.VMEM((2, HALO + 2 * REACH, per, 2 * members, LANES), jnp.float32),
            pltpu.VMEM((2, HALO, per, 2 * members, LANES), jnp.float32),
            pltpu.VMEM((2, members, TILE, width), jnp.float32),
            pltpu.SMEM((2, HALO, LANES), jnp.float32),
            pltpu.SemaphoreType.DMA((4,)),
        ],
        input_output_aliases={6: 0},
        compiler_params=grant(6),
    )(offsets, fractions, factors, before, after, main, pltpu.with_memory_space_constraint(done, pltpu.HBM))


def from_neighbours(first, last, axis):
    peers = lax.axis_size(axis)
    forth = [(i, i + 1) for i in range(peers - 1)]
    back = [(j, i) for i, j in forth]
    return lax.ppermute(last, axis, forth), lax.ppermute(first, axis, back)


def shards(fields, offsets, fractions, coefs):
    shape = fields.shape
    rows, width = shape[2], shape[3]
    blocks = fields.reshape(-1, rows, width)
    factors = coefs / 12.0
    main = lax.all_to_all(blocks, "azi", 0, 0, tiled=True)

    table = jnp.concatenate([offsets.astype(jnp.float32), fractions, factors[None]]).T
    table = jnp.stack([table[:HALO], table[rows - HALO :]])
    table = jnp.pad(table, ((0, 0), (0, 0), (0, width - table.shape[2])))

    before, after = from_neighbours(*edge_radii(main, table), "rad")
    done = inner(offsets, fractions, factors, main)
    done = edges(offsets, fractions, factors, before, after, main, done)
    return lax.all_to_all(done, "azi", 0, 0, tiled=True).reshape(shape)


def solution(mesh):
    placed = (P(None, None, "rad", "azi"), P(None, "rad"), P(None, "rad"), P("rad"))
    return jax.shard_map(
        shards, mesh=mesh, in_specs=placed, out_specs=P(None, None, "rad", "azi"), check_vma=False
    )
```

```python
import functools

import jax
import jax.numpy as jnp
from jax import lax
from jax.experimental import pallas as pl
from jax.experimental.pallas import tpu as pltpu
from jax.sharding import PartitionSpec as P

LANES = 128
REACH = 2
HALO = 2 * REACH
RELAY, FIRST, GROUP = 16, 60, 8


def diffused(far_up, up, here, down, far_down, factor):
    return here + factor * (16.0 * (up + down) - (far_up + far_down) - 30.0 * here)


def partly_shifted(row, shift, weight):
    part = shift & (LANES - 1)
    lane = lax.broadcasted_iota(jnp.int32, row[0].shape, 1)
    own_first, own_behind = lane >= part, lane > part
    first = [pltpu.roll(line, part, 1) for line in row]
    behind = [pltpu.roll(line, (part + 1) & (LANES - 1), 1) for line in row]
    first = [pltpu.roll(first[-1], 1, 0)] + first
    behind = [pltpu.roll(behind[-1], 1, 0)] + behind
    return [
        (1.0 - weight) * jnp.where(own_first, first[c + 1], first[c])
        + weight * jnp.where(own_behind, behind[c + 1], behind[c])
        for c in range(len(row))
    ]


def keep(ref, i, row):
    blocks = row[0].shape[0]
    for c, line in enumerate(row):
        ref[i, c, pl.ds(0, blocks)] = line
        ref[i, c, pl.ds(blocks, blocks)] = line


def moved_line(ref, i, shift, c):
    per, blocks = ref.shape[1], ref.shape[2] // 2
    lines = shift >> 7
    some, whole = lines & (per - 1), lines >> (per.bit_length() - 1)
    wraps = (c < some).astype(jnp.int32)
    return ref[i, c - some + wraps * per, pl.ds(blocks - whole - wraps, blocks)]


def moved(ref, i, shift):
    return [moved_line(ref, i, shift, c) for c in range(ref.shape[1])]


def in_groups(count, size, body):
    size = next(s for s in range(size, 0, -1) if count % s == 0)

    def group(t, carry):
        body(t * size, size)
        return carry

    lax.fori_loop(0, count // size, group, 0)


def two_steps(offset, fraction, factor, grid, once, twice):
    per = grid.shape[1]

    def diffuse(start, size, at, number, line, out):
        rows = [[] for _ in range(size)]
        for c in range(per):
            read = [line(start + j, c) for j in range(size + 2 * REACH)]
            for u in range(size):
                rows[u].append(diffused(*read[u : u + 2 * REACH + 1], factor(start + u + at)))
        for u in range(size):
            here = start + u + at
            keep(out, start + u, partly_shifted(rows[u], offset(number, here), fraction(number, here)))

    def first_step(start, size):
        diffuse(start, size, REACH, 0, lambda i, c: grid[i, c], once)

    def second_step(start, size):
        diffuse(start, size, HALO, 1, lambda i, c: moved_line(once, i, offset(0, i + REACH), c), twice)

    return first_step, second_step


def write(offset, twice, start, count, out, to):
    for i in range(count):
        out[:, to + i, :] = jnp.concatenate(moved(twice, start + i, offset(start + i)), axis=1)


def load(grid, at, source, row, turn=0):
    line = source[pl.ds(0, grid.shape[2]), row, :]
    if turn:
        line = jnp.concatenate([line[turn:], line[:turn]])
    for c in range(grid.shape[1]):
        grid[at, c] = line[:, c * LANES : (c + 1) * LANES]


def edge_radii_kernel(main, table, first, last):
    members, rows, _ = main.shape
    first[pl.ds(0, members)] = main[:, :HALO]
    first[members] = table[0]
    last[pl.ds(0, members)] = main[:, rows - HALO :]
    last[members] = table[1]


def inner_kernel(offsets, fractions, factors, main, out, grid, once, twice):
    rows = main.shape[1]

    def relay(start, size):
        for u in range(size):
            load(grid, start + u, main, start + u)

    first_step, second_step = two_steps(
        lambda step, at: offsets[step, at],
        lambda step, at: fractions[step, at],
        lambda at: factors[at],
        grid,
        once,
        twice,
    )
    in_groups(rows, RELAY, relay)
    in_groups(rows - 2 * REACH, FIRST, first_step)
    for lo in range(HALO, rows - HALO, GROUP):
        second_step(lo - HALO, GROUP)
        write(lambda i: offsets[1, i + HALO], twice, lo - HALO, GROUP, out, lo)


def edge_kernel(offsets, fractions, factors, before, after, main, given, out, grid, once, twice, table, sems):
    del given
    members, rows, _ = main.shape
    steps = offsets.shape[0]
    tables = [
        pltpu.make_async_copy(halo.at[members, :, pl.ds(0, LANES)], table.at[side], sems.at[side])
        for side, halo in enumerate((before, after))
    ]
    for copy in tables:
        copy.start()

    for side, halo in enumerate((before, after)):
        for r in range(HALO):
            load(grid.at[side], r + side * 2 * HALO, halo, r, members // 2)
        for r in range(2 * HALO):
            load(grid.at[side], r + (1 - side) * HALO, main, r + side * (rows - 2 * HALO))
    for copy in tables:
        copy.wait()

    def side_steps(side):
        def entry(own, column, at):
            row = at - HALO if side == 0 else at + rows - 2 * HALO
            if 0 <= row < rows:
                return own(row)
            return table[side, row + HALO if side == 0 else row - rows, column]

        def offset(step, at):
            return entry(lambda row: offsets[step, row], step, at).astype(jnp.int32)

        def fraction(step, at):
            return entry(lambda row: fractions[step, row], steps + step, at)

        def factor(at):
            return entry(lambda row: factors[row], 2 * steps, at)

        first_step, second_step = two_steps(offset, fraction, factor, grid.at[side], once.at[side], twice.at[side])
        return offset, first_step, second_step

    sides = [side_steps(side) for side in range(2)]
    for _, first_step, _ in sides:
        first_step(0, HALO + 2 * REACH)
    for _, _, second_step in sides:
        second_step(0, HALO)
    for side, (offset, _, _) in enumerate(sides):
        whole = functools.partial(offset, 1)
        write(lambda i, whole=whole: whole(i + HALO), twice.at[side], 0, HALO, out, side * (rows - HALO))


SMEM = pl.BlockSpec(memory_space=pltpu.SMEM)
VMEM = pl.BlockSpec(memory_space=pltpu.VMEM)


def grant(mebibytes):
    return pltpu.CompilerParams(vmem_limit_bytes=mebibytes << 20)


def edge_radii(main, table):
    members, _, width = main.shape
    side = jax.ShapeDtypeStruct((members + 1, HALO, width), jnp.float32)
    return pl.pallas_call(
        edge_radii_kernel,
        out_shape=[side, side],
        in_specs=[VMEM, VMEM],
        out_specs=[VMEM, VMEM],
        compiler_params=grant(2),
    )(main, table)


def inner(offsets, fractions, factors, main):
    members, rows, width = main.shape
    per = width // LANES
    return pl.pallas_call(
        inner_kernel,
        out_shape=pltpu.VMEM(main.shape, jnp.float32),
        in_specs=[SMEM] * 3 + [VMEM],
        out_specs=VMEM,
        scratch_shapes=[
            pltpu.VMEM((rows, per, members, LANES), jnp.float32),
            pltpu.VMEM((rows - 2 * REACH, per, 2 * members, LANES), jnp.float32),
            pltpu.VMEM((rows - 2 * HALO, per, 2 * members, LANES), jnp.float32),
        ],
        compiler_params=grant(16),
    )(offsets, fractions, factors, main)


def edges(offsets, fractions, factors, before, after, main, done):
    members, _, width = main.shape
    per = width // LANES
    return pl.pallas_call(
        edge_kernel,
        out_shape=pltpu.VMEM(main.shape, jnp.float32),
        in_specs=[SMEM] * 3 + [VMEM] * 4,
        out_specs=VMEM,
        scratch_shapes=[
            pltpu.VMEM((2, 3 * HALO, per, members, LANES), jnp.float32),
            pltpu.VMEM((2, HALO + 2 * REACH, per, 2 * members, LANES), jnp.float32),
            pltpu.VMEM((2, HALO, per, 2 * members, LANES), jnp.float32),
            pltpu.SMEM((2, HALO, LANES), jnp.float32),
            pltpu.SemaphoreType.DMA((2,)),
        ],
        input_output_aliases={6: 0},
        compiler_params=grant(6),
    )(offsets, fractions, factors, before, after, main, pltpu.with_memory_space_constraint(done, pltpu.VMEM))


def owners(parts, members):
    half = members // 2
    return [[part * members + (m + part % 2 * half) % members for m in range(members)] for part in range(parts)]


def exchanged(blocks, devices):
    return lax.all_to_all(blocks, ("rad", "azi"), 0, 0, axis_index_groups=devices, tiled=True)


def from_neighbours(first, last, devices):
    forth = [pair for part, after in zip(devices, devices[1:]) for pair in zip(part, after)]
    back = [(j, i) for i, j in forth]
    return lax.ppermute(last, ("rad", "azi"), forth), lax.ppermute(first, ("rad", "azi"), back)


def shards(fields, offsets, fractions, coefs):
    shape = fields.shape
    rows, width = shape[2], shape[3]
    blocks = fields.reshape(-1, rows, width)
    factors = coefs / 12.0
    devices = owners(lax.axis_size("rad"), lax.axis_size("azi"))
    main = exchanged(blocks, devices)

    table = jnp.concatenate([offsets.astype(jnp.float32), fractions, factors[None]]).T
    table = jnp.stack([table[:HALO], table[rows - HALO :]])
    table = jnp.pad(table, ((0, 0), (0, 0), (0, width - table.shape[2])))

    before, after = from_neighbours(*edge_radii(main, table), devices)
    done = inner(offsets, fractions, factors, main)
    done = edges(offsets, fractions, factors, before, after, main, done)
    return exchanged(done, devices).reshape(shape)


def solution(mesh):
    placed = (P(None, None, "rad", "azi"), P(None, "rad"), P(None, "rad"), P("rad"))
    return jax.shard_map(
        shards, mesh=mesh, in_specs=placed, out_specs=P(None, None, "rad", "azi"), check_vma=False
    )
```

```python
import functools

import jax
import jax.numpy as jnp
from jax import lax
from jax.experimental import pallas as pl
from jax.experimental.pallas import tpu as pltpu
from jax.sharding import PartitionSpec as P

LANES = 128
REACH = 2
HALO = 2 * REACH
RELAY, FIRST, GROUP = 16, 60, 8


def diffused(far_up, up, here, down, far_down, factor):
    return here + factor * (16.0 * (up + down) - (far_up + far_down) - 30.0 * here)


def partly_shifted(row, shift, weight):
    part = shift & (LANES - 1)
    lane = lax.broadcasted_iota(jnp.int32, row[0].shape, 1)
    own_first, own_behind = lane >= part, lane > part
    first = [pltpu.roll(line, part, 1) for line in row]
    behind = [pltpu.roll(line, (part + 1) & (LANES - 1), 1) for line in row]
    first = [pltpu.roll(first[-1], 1, 0)] + first
    behind = [pltpu.roll(behind[-1], 1, 0)] + behind
    return [
        (1.0 - weight) * jnp.where(own_first, first[c + 1], first[c])
        + weight * jnp.where(own_behind, behind[c + 1], behind[c])
        for c in range(len(row))
    ]


def keep(ref, i, row):
    blocks = row[0].shape[0]
    for c, line in enumerate(row):
        ref[i, c, pl.ds(0, blocks)] = line
        ref[i, c, pl.ds(blocks, blocks)] = line


def moved_line(ref, i, shift, c):
    per, blocks = ref.shape[1], ref.shape[2] // 2
    lines = shift >> 7
    some, whole = lines & (per - 1), lines >> (per.bit_length() - 1)
    wraps = (c < some).astype(jnp.int32)
    return ref[i, c - some + wraps * per, pl.ds(blocks - whole - wraps, blocks)]


def moved(ref, i, shift):
    return [moved_line(ref, i, shift, c) for c in range(ref.shape[1])]


def in_groups(count, size, body):
    size = next(s for s in range(size, 0, -1) if count % s == 0)

    def group(t, carry):
        body(t * size, size)
        return carry

    lax.fori_loop(0, count // size, group, 0)


def two_steps(offset, fraction, factor, grid, once, twice):
    per = grid.shape[1]

    def diffuse(start, size, at, number, line, out):
        rows = [[] for _ in range(size)]
        for c in range(per):
            read = [line(start + j, c) for j in range(size + 2 * REACH)]
            for u in range(size):
                rows[u].append(diffused(*read[u : u + 2 * REACH + 1], factor(start + u + at)))
        for u in range(size):
            here = start + u + at
            keep(out, start + u, partly_shifted(rows[u], offset(number, here), fraction(number, here)))

    def first_step(start, size):
        diffuse(start, size, REACH, 0, lambda i, c: grid[i, c], once)

    def second_step(start, size):
        diffuse(start, size, HALO, 1, lambda i, c: moved_line(once, i, offset(0, i + REACH), c), twice)

    return first_step, second_step


def write(offset, twice, start, count, out, to):
    for i in range(count):
        out[:, to + i, :] = jnp.concatenate(moved(twice, start + i, offset(start + i)), axis=1)


def load(grid, at, source, row, turn=0):
    line = source[pl.ds(0, grid.shape[2]), row, :]
    if turn:
        line = jnp.concatenate([line[turn:], line[:turn]])
    for c in range(grid.shape[1]):
        grid[at, c] = line[:, c * LANES : (c + 1) * LANES]


def edge_radii_kernel(inside, main, table, first, last):
    members, rows, _ = main.shape
    for side, (out, start) in enumerate(((first, 0), (last, rows - HALO))):
        sent = inside[side] > 0
        radii = main[:, start : start + HALO]
        out[pl.ds(0, members)] = jnp.where(sent, radii, jnp.zeros_like(radii))
        out[members] = jnp.where(sent, table[side], jnp.zeros_like(table[side]))


def inner_kernel(offsets, fractions, factors, main, out, grid, once, twice):
    rows = main.shape[1]

    def relay(start, size):
        for u in range(size):
            load(grid, start + u, main, start + u)

    first_step, second_step = two_steps(
        lambda step, at: offsets[step, at],
        lambda step, at: fractions[step, at],
        lambda at: factors[at],
        grid,
        once,
        twice,
    )
    in_groups(rows, RELAY, relay)
    in_groups(rows - 2 * REACH, FIRST, first_step)
    for lo in range(HALO, rows - HALO, GROUP):
        second_step(lo - HALO, GROUP)
        write(lambda i: offsets[1, i + HALO], twice, lo - HALO, GROUP, out, lo)


def edge_kernel(offsets, fractions, factors, before, after, main, given, out, grid, once, twice, table, sems):
    del given
    members, rows, _ = main.shape
    steps = offsets.shape[0]
    tables = [
        pltpu.make_async_copy(halo.at[members, :, pl.ds(0, LANES)], table.at[side], sems.at[side])
        for side, halo in enumerate((before, after))
    ]
    for copy in tables:
        copy.start()

    for side, halo in enumerate((before, after)):
        for r in range(HALO):
            load(grid.at[side], r + side * 2 * HALO, halo, r, members // 2)
        for r in range(2 * HALO):
            load(grid.at[side], r + (1 - side) * HALO, main, r + side * (rows - 2 * HALO))
    for copy in tables:
        copy.wait()

    def side_steps(side):
        def entry(own, column, at):
            row = at - HALO if side == 0 else at + rows - 2 * HALO
            if 0 <= row < rows:
                return own(row)
            return table[side, row + HALO if side == 0 else row - rows, column]

        def offset(step, at):
            return entry(lambda row: offsets[step, row], step, at).astype(jnp.int32)

        def fraction(step, at):
            return entry(lambda row: fractions[step, row], steps + step, at)

        def factor(at):
            return entry(lambda row: factors[row], 2 * steps, at)

        first_step, second_step = two_steps(offset, fraction, factor, grid.at[side], once.at[side], twice.at[side])
        return offset, first_step, second_step

    sides = [side_steps(side) for side in range(2)]
    for _, first_step, _ in sides:
        first_step(0, HALO + 2 * REACH)
    for _, _, second_step in sides:
        second_step(0, HALO)
    for side, (offset, _, _) in enumerate(sides):
        whole = functools.partial(offset, 1)
        write(lambda i, whole=whole: whole(i + HALO), twice.at[side], 0, HALO, out, side * (rows - HALO))


SMEM = pl.BlockSpec(memory_space=pltpu.SMEM)
VMEM = pl.BlockSpec(memory_space=pltpu.VMEM)


def grant(mebibytes):
    return pltpu.CompilerParams(vmem_limit_bytes=mebibytes << 20)


def edge_radii(inside, main, table):
    members, _, width = main.shape
    side = jax.ShapeDtypeStruct((members + 1, HALO, width), jnp.float32)
    return pl.pallas_call(
        edge_radii_kernel,
        out_shape=[side, side],
        in_specs=[SMEM, VMEM, VMEM],
        out_specs=[VMEM, VMEM],
        compiler_params=grant(2),
    )(inside, main, table)


def inner(offsets, fractions, factors, main):
    members, rows, width = main.shape
    per = width // LANES
    return pl.pallas_call(
        inner_kernel,
        out_shape=pltpu.VMEM(main.shape, jnp.float32),
        in_specs=[SMEM] * 3 + [VMEM],
        out_specs=VMEM,
        scratch_shapes=[
            pltpu.VMEM((rows, per, members, LANES), jnp.float32),
            pltpu.VMEM((rows - 2 * REACH, per, 2 * members, LANES), jnp.float32),
            pltpu.VMEM((rows - 2 * HALO, per, 2 * members, LANES), jnp.float32),
        ],
        compiler_params=grant(16),
    )(offsets, fractions, factors, main)


def edges(offsets, fractions, factors, before, after, main, done):
    members, _, width = main.shape
    per = width // LANES
    return pl.pallas_call(
        edge_kernel,
        out_shape=pltpu.VMEM(main.shape, jnp.float32),
        in_specs=[SMEM] * 3 + [VMEM] * 4,
        out_specs=VMEM,
        scratch_shapes=[
            pltpu.VMEM((2, 3 * HALO, per, members, LANES), jnp.float32),
            pltpu.VMEM((2, HALO + 2 * REACH, per, 2 * members, LANES), jnp.float32),
            pltpu.VMEM((2, HALO, per, 2 * members, LANES), jnp.float32),
            pltpu.SMEM((2, HALO, LANES), jnp.float32),
            pltpu.SemaphoreType.DMA((2,)),
        ],
        input_output_aliases={6: 0},
        compiler_params=grant(6),
    )(offsets, fractions, factors, before, after, main, pltpu.with_memory_space_constraint(done, pltpu.VMEM))


def owners(parts, members):
    half = members // 2
    return [[part * members + (m + part % 2 * half) % members for m in range(members)] for part in range(parts)]


def exchanged(blocks, devices):
    return lax.all_to_all(blocks, ("rad", "azi"), 0, 0, axis_index_groups=devices, tiled=True)


def from_neighbours(first, last, devices):
    forth = [pair for part, after in zip(devices, devices[1:] + devices[:1]) for pair in zip(part, after)]
    back = [(j, i) for i, j in forth]
    return lax.ppermute(last, ("rad", "azi"), forth), lax.ppermute(first, ("rad", "azi"), back)


def shards(fields, offsets, fractions, coefs):
    shape = fields.shape
    rows, width = shape[2], shape[3]
    blocks = fields.reshape(-1, rows, width)
    factors = coefs / 12.0
    devices = owners(lax.axis_size("rad"), lax.axis_size("azi"))
    main = exchanged(blocks, devices)

    table = jnp.concatenate([offsets.astype(jnp.float32), fractions, factors[None]]).T
    table = jnp.stack([table[:HALO], table[rows - HALO :]])
    table = jnp.pad(table, ((0, 0), (0, 0), (0, width - table.shape[2])))

    part = lax.axis_index("rad")
    inside = jnp.stack([part > 0, part < len(devices) - 1]).astype(jnp.int32)
    before, after = from_neighbours(*edge_radii(inside, main, table), devices)
    done = inner(offsets, fractions, factors, main)
    done = edges(offsets, fractions, factors, before, after, main, done)
    return exchanged(done, devices).reshape(shape)


def solution(mesh):
    placed = (P(None, None, "rad", "azi"), P(None, "rad"), P(None, "rad"), P("rad"))
    return jax.shard_map(
        shards, mesh=mesh, in_specs=placed, out_specs=P(None, None, "rad", "azi"), check_vma=False
    )
```

```python
import functools

import jax
import jax.numpy as jnp
from jax import lax
from jax.experimental import pallas as pl
from jax.experimental.pallas import tpu as pltpu
from jax.sharding import PartitionSpec as P

LANES = 128
REACH = 2
HALO = 2 * REACH
PER_DIFFERENCE = 1.0 / 12.0
RELAY, FIRST, GROUP = 16, 60, 8


def diffused(far_up, up, here, down, far_down, factor):
    return here + factor * (16.0 * (up + down) - (far_up + far_down) - 30.0 * here)


def partly_shifted(row, shift, weight):
    part = shift & (LANES - 1)
    lane = lax.broadcasted_iota(jnp.int32, row[0].shape, 1)
    own_first, own_behind = lane >= part, lane > part
    first = [pltpu.roll(line, part, 1) for line in row]
    behind = [pltpu.roll(line, (part + 1) & (LANES - 1), 1) for line in row]
    first = [pltpu.roll(first[-1], 1, 0)] + first
    behind = [pltpu.roll(behind[-1], 1, 0)] + behind
    return [
        (1.0 - weight) * jnp.where(own_first, first[c + 1], first[c])
        + weight * jnp.where(own_behind, behind[c + 1], behind[c])
        for c in range(len(row))
    ]


def keep(ref, i, row):
    blocks = row[0].shape[0]
    for c, line in enumerate(row):
        ref[i, c, pl.ds(0, blocks)] = line
        ref[i, c, pl.ds(blocks, blocks)] = line


def moved_line(ref, i, shift, c):
    per, blocks = ref.shape[1], ref.shape[2] // 2
    lines = shift >> 7
    some, whole = lines & (per - 1), lines >> (per.bit_length() - 1)
    wraps = (c < some).astype(jnp.int32)
    return ref[i, c - some + wraps * per, pl.ds(blocks - whole - wraps, blocks)]


def moved(ref, i, shift):
    return [moved_line(ref, i, shift, c) for c in range(ref.shape[1])]


def in_groups(count, size, body):
    size = next(s for s in range(size, 0, -1) if count % s == 0)

    def group(t, carry):
        body(t * size, size)
        return carry

    lax.fori_loop(0, count // size, group, 0)


def two_steps(offset, fraction, factor, grid, once, twice):
    per = grid.shape[1]

    def diffuse(start, size, at, number, line, out):
        rows = [[] for _ in range(size)]
        for c in range(per):
            read = [line(start + j, c) for j in range(size + 2 * REACH)]
            for u in range(size):
                rows[u].append(diffused(*read[u : u + 2 * REACH + 1], factor(start + u + at)))
        for u in range(size):
            here = start + u + at
            keep(out, start + u, partly_shifted(rows[u], offset(number, here), fraction(number, here)))

    def first_step(start, size):
        diffuse(start, size, REACH, 0, lambda i, c: grid[i, c], once)

    def second_step(start, size):
        diffuse(start, size, HALO, 1, lambda i, c: moved_line(once, i, offset(0, i + REACH), c), twice)

    return first_step, second_step


def write(offset, twice, start, count, out, to):
    for i in range(count):
        out[:, to + i, :] = jnp.concatenate(moved(twice, start + i, offset(start + i)), axis=1)


def load(grid, at, source, row, turn=0):
    line = source[pl.ds(0, grid.shape[2]), row, :]
    if turn:
        line = jnp.concatenate([line[turn:], line[:turn]])
    for c in range(grid.shape[1]):
        grid[at, c] = line[:, c * LANES : (c + 1) * LANES]


def edge_radii_kernel(offsets, fractions, coefs, main, first, last):
    members, rows, width = main.shape
    steps = offsets.shape[0]
    part, parts = lax.axis_index("rad"), lax.axis_size("rad")
    lane = lax.broadcasted_iota(jnp.int32, (1, width), 1)
    for out, start, sent in ((first, 0, part > 0), (last, rows - HALO, part < parts - 1)):
        radii = main[:, start : start + HALO]
        out[pl.ds(0, members)] = jnp.where(sent, radii, jnp.zeros_like(radii))
        for r in range(HALO):
            at = start + r
            entries = [offsets[step, at].astype(jnp.float32) for step in range(steps)]
            entries += [fractions[step, at] for step in range(steps)]
            entries.append(coefs[at])
            line = jnp.zeros((1, width), jnp.float32)
            for column, entry in enumerate(entries):
                line = jnp.where(lane == column, jnp.where(sent, entry, 0.0), line)
            out[members, pl.ds(r, 1)] = line


def inner_kernel(offsets, fractions, coefs, main, out, grid, once, twice):
    rows = main.shape[1]

    def relay(start, size):
        for u in range(size):
            load(grid, start + u, main, start + u)

    first_step, second_step = two_steps(
        lambda step, at: offsets[step, at],
        lambda step, at: fractions[step, at],
        lambda at: coefs[at] * PER_DIFFERENCE,
        grid,
        once,
        twice,
    )
    in_groups(rows, RELAY, relay)
    in_groups(rows - 2 * REACH, FIRST, first_step)
    for lo in range(HALO, rows - HALO, GROUP):
        second_step(lo - HALO, GROUP)
        write(lambda i: offsets[1, i + HALO], twice, lo - HALO, GROUP, out, lo)


def edge_kernel(offsets, fractions, coefs, before, after, main, given, out, grid, once, twice, table, sems):
    del given
    members, rows, _ = main.shape
    steps = offsets.shape[0]
    tables = [
        pltpu.make_async_copy(halo.at[members, :, pl.ds(0, LANES)], table.at[side], sems.at[side])
        for side, halo in enumerate((before, after))
    ]
    for copy in tables:
        copy.start()

    for side, halo in enumerate((before, after)):
        for r in range(HALO):
            load(grid.at[side], r + side * 2 * HALO, halo, r, members // 2)
        for r in range(2 * HALO):
            load(grid.at[side], r + (1 - side) * HALO, main, r + side * (rows - 2 * HALO))
    for copy in tables:
        copy.wait()

    def side_steps(side):
        def entry(own, column, at):
            row = at - HALO if side == 0 else at + rows - 2 * HALO
            if 0 <= row < rows:
                return own(row)
            return table[side, row + HALO if side == 0 else row - rows, column]

        def offset(step, at):
            return entry(lambda row: offsets[step, row], step, at).astype(jnp.int32)

        def fraction(step, at):
            return entry(lambda row: fractions[step, row], steps + step, at)

        def factor(at):
            return entry(lambda row: coefs[row], 2 * steps, at) * PER_DIFFERENCE

        first_step, second_step = two_steps(offset, fraction, factor, grid.at[side], once.at[side], twice.at[side])
        return offset, first_step, second_step

    sides = [side_steps(side) for side in range(2)]
    for _, first_step, _ in sides:
        first_step(0, HALO + 2 * REACH)
    for _, _, second_step in sides:
        second_step(0, HALO)
    for side, (offset, _, _) in enumerate(sides):
        whole = functools.partial(offset, 1)
        write(lambda i, whole=whole: whole(i + HALO), twice.at[side], 0, HALO, out, side * (rows - HALO))


SMEM = pl.BlockSpec(memory_space=pltpu.SMEM)
VMEM = pl.BlockSpec(memory_space=pltpu.VMEM)


def grant(mebibytes):
    return pltpu.CompilerParams(vmem_limit_bytes=mebibytes << 20)


def edge_radii(offsets, fractions, coefs, main):
    members, _, width = main.shape
    side = jax.ShapeDtypeStruct((members + 1, HALO, width), jnp.float32)
    return pl.pallas_call(
        edge_radii_kernel,
        out_shape=[side, side],
        in_specs=[SMEM] * 3 + [VMEM],
        out_specs=[VMEM, VMEM],
        compiler_params=grant(2),
    )(offsets, fractions, coefs, main)


def inner(offsets, fractions, coefs, main):
    members, rows, width = main.shape
    per = width // LANES
    return pl.pallas_call(
        inner_kernel,
        out_shape=pltpu.VMEM(main.shape, jnp.float32),
        in_specs=[SMEM] * 3 + [VMEM],
        out_specs=VMEM,
        scratch_shapes=[
            pltpu.VMEM((rows, per, members, LANES), jnp.float32),
            pltpu.VMEM((rows - 2 * REACH, per, 2 * members, LANES), jnp.float32),
            pltpu.VMEM((rows - 2 * HALO, per, 2 * members, LANES), jnp.float32),
        ],
        compiler_params=grant(16),
    )(offsets, fractions, coefs, main)


def edges(offsets, fractions, coefs, before, after, main, done):
    members, _, width = main.shape
    per = width // LANES
    return pl.pallas_call(
        edge_kernel,
        out_shape=pltpu.VMEM(main.shape, jnp.float32),
        in_specs=[SMEM] * 3 + [VMEM] * 4,
        out_specs=VMEM,
        scratch_shapes=[
            pltpu.VMEM((2, 3 * HALO, per, members, LANES), jnp.float32),
            pltpu.VMEM((2, HALO + 2 * REACH, per, 2 * members, LANES), jnp.float32),
            pltpu.VMEM((2, HALO, per, 2 * members, LANES), jnp.float32),
            pltpu.SMEM((2, HALO, LANES), jnp.float32),
            pltpu.SemaphoreType.DMA((2,)),
        ],
        input_output_aliases={6: 0},
        compiler_params=grant(6),
    )(offsets, fractions, coefs, before, after, main, pltpu.with_memory_space_constraint(done, pltpu.VMEM))


def owners(parts, members):
    half = members // 2
    return [[part * members + (m + part % 2 * half) % members for m in range(members)] for part in range(parts)]


def exchanged(blocks, devices):
    return lax.all_to_all(blocks, ("rad", "azi"), 0, 0, axis_index_groups=devices, tiled=True)


def from_neighbours(first, last, devices):
    forth = [pair for part, after in zip(devices, devices[1:] + devices[:1]) for pair in zip(part, after)]
    back = [(j, i) for i, j in forth]
    return lax.ppermute(last, ("rad", "azi"), forth), lax.ppermute(first, ("rad", "azi"), back)


def shards(fields, offsets, fractions, coefs):
    shape = fields.shape
    rows, width = shape[2], shape[3]
    blocks = fields.reshape(-1, rows, width)
    devices = owners(lax.axis_size("rad"), lax.axis_size("azi"))
    main = exchanged(blocks, devices)

    before, after = from_neighbours(*edge_radii(offsets, fractions, coefs, main), devices)
    done = inner(offsets, fractions, coefs, main)
    done = edges(offsets, fractions, coefs, before, after, main, done)
    return exchanged(done, devices).reshape(shape)


def solution(mesh):
    placed = (P(None, None, "rad", "azi"), P(None, "rad"), P(None, "rad"), P("rad"))
    return jax.shard_map(
        shards, mesh=mesh, in_specs=placed, out_specs=P(None, None, "rad", "azi"), check_vma=False
    )
```

```python
import functools

import jax
import jax.numpy as jnp
from jax import lax
from jax.experimental import pallas as pl
from jax.experimental.pallas import tpu as pltpu
from jax.sharding import PartitionSpec as P

LANES = 128
REACH = 2
HALO = 2 * REACH
PER_DIFFERENCE = 1.0 / 12.0
RELAY, FIRST, GROUP = 16, 60, 8


def diffused(far_up, up, here, down, far_down, factor):
    return here + factor * (16.0 * (up + down) - (far_up + far_down) - 30.0 * here)


def partly_shifted(row, shift, weight):
    part = shift & (LANES - 1)
    lane = lax.broadcasted_iota(jnp.int32, row[0].shape, 1)
    own_first, own_behind = lane >= part, lane > part
    first = [pltpu.roll(line, part, 1) for line in row]
    behind = [pltpu.roll(line, (part + 1) & (LANES - 1), 1) for line in row]
    first = [pltpu.roll(first[-1], 1, 0)] + first
    behind = [pltpu.roll(behind[-1], 1, 0)] + behind
    return [
        (1.0 - weight) * jnp.where(own_first, first[c + 1], first[c])
        + weight * jnp.where(own_behind, behind[c + 1], behind[c])
        for c in range(len(row))
    ]


def keep(ref, i, row):
    blocks = row[0].shape[0]
    for c, line in enumerate(row):
        ref[i, c, pl.ds(0, blocks)] = line
        ref[i, c, pl.ds(blocks, blocks)] = line


def moved_line(ref, i, shift, c):
    per, blocks = ref.shape[1], ref.shape[2] // 2
    lines = shift >> 7
    some, whole = lines & (per - 1), lines >> (per.bit_length() - 1)
    wraps = (c < some).astype(jnp.int32)
    return ref[i, c - some + wraps * per, pl.ds(blocks - whole - wraps, blocks)]


def moved(ref, i, shift):
    return [moved_line(ref, i, shift, c) for c in range(ref.shape[1])]


def in_groups(count, size, body):
    size = next(s for s in range(size, 0, -1) if count % s == 0)

    def group(t, carry):
        body(t * size, size)
        return carry

    lax.fori_loop(0, count // size, group, 0)


def two_steps(offset, fraction, factor, grid, once, twice):
    per = grid.shape[1]

    def diffuse(start, size, at, number, line, out):
        rows = [[] for _ in range(size)]
        for c in range(per):
            read = [line(start + j, c) for j in range(size + 2 * REACH)]
            for u in range(size):
                rows[u].append(diffused(*read[u : u + 2 * REACH + 1], factor(start + u + at)))
        for u in range(size):
            here = start + u + at
            keep(out, start + u, partly_shifted(rows[u], offset(number, here), fraction(number, here)))

    def first_step(start, size):
        diffuse(start, size, REACH, 0, lambda i, c: grid[i, c], once)

    def second_step(start, size):
        diffuse(start, size, HALO, 1, lambda i, c: moved_line(once, i, offset(0, i + REACH), c), twice)

    return first_step, second_step


def write(offset, twice, start, count, out, to):
    for i in range(count):
        out[:, to + i, :] = jnp.concatenate(moved(twice, start + i, offset(start + i)), axis=1)


def load(grid, at, source, row, turn=0):
    line = source[pl.ds(0, grid.shape[2]), row, :]
    if turn:
        line = jnp.concatenate([line[turn:], line[:turn]])
    for c in range(grid.shape[1]):
        grid[at, c] = line[:, c * LANES : (c + 1) * LANES]


def edge_radii_kernel(offsets, fractions, coefs, main, first, last):
    members, rows, width = main.shape
    steps = offsets.shape[0]
    part, parts = lax.axis_index("rad"), lax.axis_size("rad")
    lane = lax.broadcasted_iota(jnp.int32, (1, width), 1)
    for out, start, sent in ((first, 0, part > 0), (last, rows - HALO, part < parts - 1)):
        radii = main[:, start : start + HALO]
        out[pl.ds(0, members)] = jnp.where(sent, radii, jnp.zeros_like(radii))
        for r in range(HALO):
            at = start + r
            entries = [offsets[step, at].astype(jnp.float32) for step in range(steps)]
            entries += [fractions[step, at] for step in range(steps)]
            entries.append(coefs[at])
            line = jnp.zeros((1, width), jnp.float32)
            for column, entry in enumerate(entries):
                line = jnp.where(lane == column, jnp.where(sent, entry, 0.0), line)
            out[members, pl.ds(r, 1)] = line


def inner_kernel(offsets, fractions, coefs, main, out, grid, once, twice):
    rows = main.shape[1]

    def relay(start, size):
        for u in range(size):
            load(grid, start + u, main, start + u)

    first_step, second_step = two_steps(
        lambda step, at: offsets[step, at],
        lambda step, at: fractions[step, at],
        lambda at: coefs[at] * PER_DIFFERENCE,
        grid,
        once,
        twice,
    )
    in_groups(rows, RELAY, relay)
    in_groups(rows - 2 * REACH, FIRST, first_step)
    for lo in range(HALO, rows - HALO, GROUP):
        second_step(lo - HALO, GROUP)
        write(lambda i: offsets[1, i + HALO], twice, lo - HALO, GROUP, out, lo)


def edge_kernel(side, offsets, fractions, coefs, halo, main, given, out, grid, once, twice, table, sem):
    del given
    members, rows, _ = main.shape
    steps = offsets.shape[0]
    copy = pltpu.make_async_copy(halo.at[members, :, pl.ds(0, LANES)], table, sem)
    copy.start()
    for r in range(HALO):
        load(grid, r + side * 2 * HALO, halo, r, members // 2)
    for r in range(2 * HALO):
        load(grid, r + (1 - side) * HALO, main, r + side * (rows - 2 * HALO))

    def entry(own, column, at):
        row = at - HALO if side == 0 else at + rows - 2 * HALO
        if 0 <= row < rows:
            return own(row)
        return table[row + HALO if side == 0 else row - rows, column]

    def offset(step, at):
        return entry(lambda row: offsets[step, row], step, at).astype(jnp.int32)

    def fraction(step, at):
        return entry(lambda row: fractions[step, row], steps + step, at)

    def factor(at):
        return entry(lambda row: coefs[row], 2 * steps, at) * PER_DIFFERENCE

    first_step, second_step = two_steps(offset, fraction, factor, grid, once, twice)
    first_step(REACH * (1 - side), HALO + REACH)
    copy.wait()
    first_step((HALO + REACH) * side, REACH)
    second_step(0, HALO)
    write(lambda i: offset(1, i + HALO), twice, 0, HALO, out, side * (rows - HALO))


SMEM = pl.BlockSpec(memory_space=pltpu.SMEM)
VMEM = pl.BlockSpec(memory_space=pltpu.VMEM)


def grant(mebibytes):
    return pltpu.CompilerParams(vmem_limit_bytes=mebibytes << 20)


def edge_radii(offsets, fractions, coefs, main):
    members, _, width = main.shape
    side = jax.ShapeDtypeStruct((members + 1, HALO, width), jnp.float32)
    return pl.pallas_call(
        edge_radii_kernel,
        out_shape=[side, side],
        in_specs=[SMEM] * 3 + [VMEM],
        out_specs=[VMEM, VMEM],
        compiler_params=grant(2),
    )(offsets, fractions, coefs, main)


def inner(offsets, fractions, coefs, main):
    members, rows, width = main.shape
    per = width // LANES
    return pl.pallas_call(
        inner_kernel,
        out_shape=pltpu.VMEM(main.shape, jnp.float32),
        in_specs=[SMEM] * 3 + [VMEM],
        out_specs=VMEM,
        scratch_shapes=[
            pltpu.VMEM((rows, per, members, LANES), jnp.float32),
            pltpu.VMEM((rows - 2 * REACH, per, 2 * members, LANES), jnp.float32),
            pltpu.VMEM((rows - 2 * HALO, per, 2 * members, LANES), jnp.float32),
        ],
        compiler_params=grant(16),
    )(offsets, fractions, coefs, main)


def edge(side, offsets, fractions, coefs, halo, main, done):
    members, _, width = main.shape
    per = width // LANES
    return pl.pallas_call(
        functools.partial(edge_kernel, side),
        out_shape=pltpu.VMEM(main.shape, jnp.float32),
        in_specs=[SMEM] * 3 + [VMEM] * 3,
        out_specs=VMEM,
        scratch_shapes=[
            pltpu.VMEM((3 * HALO, per, members, LANES), jnp.float32),
            pltpu.VMEM((HALO + 2 * REACH, per, 2 * members, LANES), jnp.float32),
            pltpu.VMEM((HALO, per, 2 * members, LANES), jnp.float32),
            pltpu.SMEM((HALO, LANES), jnp.float32),
            pltpu.SemaphoreType.DMA,
        ],
        input_output_aliases={5: 0},
        compiler_params=grant(6),
    )(offsets, fractions, coefs, halo, main, pltpu.with_memory_space_constraint(done, pltpu.VMEM))


def owners(parts, members):
    half = members // 2
    return [[part * members + (m + part % 2 * half) % members for m in range(members)] for part in range(parts)]


def exchanged(blocks, devices):
    return lax.all_to_all(blocks, ("rad", "azi"), 0, 0, axis_index_groups=devices, tiled=True)


def from_neighbours(first, last, devices):
    forth = [pair for part, after in zip(devices, devices[1:] + devices[:1]) for pair in zip(part, after)]
    back = [(j, i) for i, j in forth]
    return lax.ppermute(last, ("rad", "azi"), forth), lax.ppermute(first, ("rad", "azi"), back)


def shards(fields, offsets, fractions, coefs):
    shape = fields.shape
    rows, width = shape[2], shape[3]
    blocks = fields.reshape(-1, rows, width)
    devices = owners(lax.axis_size("rad"), lax.axis_size("azi"))
    main = exchanged(blocks, devices)

    before, after = from_neighbours(*edge_radii(offsets, fractions, coefs, main), devices)
    done = inner(offsets, fractions, coefs, main)
    for side, halo in enumerate((before, after)):
        done = edge(side, offsets, fractions, coefs, halo, main, done)
    return exchanged(done, devices).reshape(shape)


def solution(mesh):
    placed = (P(None, None, "rad", "azi"), P(None, "rad"), P(None, "rad"), P("rad"))
    return jax.shard_map(
        shards, mesh=mesh, in_specs=placed, out_specs=P(None, None, "rad", "azi"), check_vma=False
    )
```

```python
import functools

import jax
import jax.numpy as jnp
from jax import lax
from jax.experimental import pallas as pl
from jax.experimental.pallas import tpu as pltpu
from jax.sharding import PartitionSpec as P

LANES = 128
REACH = 2
HALO = 2 * REACH
PER_DIFFERENCE = 1.0 / 12.0
TILE = 8
RELAY, FIRST, GROUP = 16, 60, 8


def diffused(far_up, up, here, down, far_down, factor):
    return here + factor * (16.0 * (up + down) - (far_up + far_down) - 30.0 * here)


def partly_shifted(row, shift, weight):
    part = shift & (LANES - 1)
    lane = lax.broadcasted_iota(jnp.int32, row[0].shape, 1)
    own_first, own_behind = lane >= part, lane > part
    first = [pltpu.roll(line, part, 1) for line in row]
    behind = [pltpu.roll(line, (part + 1) & (LANES - 1), 1) for line in row]
    first = [pltpu.roll(first[-1], 1, 0)] + first
    behind = [pltpu.roll(behind[-1], 1, 0)] + behind
    return [
        (1.0 - weight) * jnp.where(own_first, first[c + 1], first[c])
        + weight * jnp.where(own_behind, behind[c + 1], behind[c])
        for c in range(len(row))
    ]


def keep(ref, i, row):
    blocks = row[0].shape[0]
    for c, line in enumerate(row):
        ref[i, c, pl.ds(0, blocks)] = line
        ref[i, c, pl.ds(blocks, blocks)] = line


def moved_line(ref, i, shift, c):
    per, blocks = ref.shape[1], ref.shape[2] // 2
    lines = shift >> 7
    some, whole = lines & (per - 1), lines >> (per.bit_length() - 1)
    wraps = (c < some).astype(jnp.int32)
    return ref[i, c - some + wraps * per, pl.ds(blocks - whole - wraps, blocks)]


def moved(ref, i, shift):
    return [moved_line(ref, i, shift, c) for c in range(ref.shape[1])]


def in_groups(count, size, body):
    size = next(s for s in range(size, 0, -1) if count % s == 0)

    def group(t, carry):
        body(t * size, size)
        return carry

    lax.fori_loop(0, count // size, group, 0)


def two_steps(offset, fraction, factor, line, once, twice):
    per = once.shape[1]

    def diffuse(start, size, at, number, line, out):
        rows = [[] for _ in range(size)]
        for c in range(per):
            read = [line(start + j, c) for j in range(size + 2 * REACH)]
            for u in range(size):
                rows[u].append(diffused(*read[u : u + 2 * REACH + 1], factor(start + u + at)))
        for u in range(size):
            here = start + u + at
            keep(out, start + u, partly_shifted(rows[u], offset(number, here), fraction(number, here)))

    def first_step(start, size):
        diffuse(start, size, REACH, 0, line, once)

    def second_step(start, size):
        diffuse(start, size, HALO, 1, lambda i, c: moved_line(once, i, offset(0, i + REACH), c), twice)

    return first_step, second_step


def write(offset, twice, start, count, out, to):
    for i in range(count):
        out[:, to + i, :] = jnp.concatenate(moved(twice, start + i, offset(start + i)), axis=1)


def load(grid, at, source, row):
    line = source[:, row, :]
    for c in range(grid.shape[1]):
        grid[at, c] = line[:, c * LANES : (c + 1) * LANES]


def edge_radii_kernel(offsets, fractions, coefs, main, first, last):
    members, rows, width = main.shape
    steps, per, half = offsets.shape[0], width // LANES, members // 2
    part, parts = lax.axis_index("rad"), lax.axis_size("rad")
    lane = lax.broadcasted_iota(jnp.int32, (1, LANES), 1)
    for out, start, sent in ((first, 0, part > 0), (last, rows - HALO, part < parts - 1)):
        for r in range(HALO):
            radius = main[:, start + r, :]
            radius = jnp.concatenate([radius[half:], radius[:half]])
            radius = jnp.where(sent, radius, jnp.zeros_like(radius))
            for c in range(per):
                out[pl.ds((r * per + c) * members, members)] = radius[:, c * LANES : (c + 1) * LANES]
        table = HALO * per * members
        out[pl.ds(table, TILE)] = jnp.zeros((TILE, LANES), jnp.float32)
        for r in range(HALO):
            at = start + r
            entries = [offsets[step, at].astype(jnp.float32) for step in range(steps)]
            entries += [fractions[step, at] for step in range(steps)]
            entries.append(coefs[at])
            line = jnp.zeros((1, LANES), jnp.float32)
            for column, entry in enumerate(entries):
                line = jnp.where(lane == column, jnp.where(sent, entry, 0.0), line)
            out[pl.ds(table + r, 1)] = line


def inner_kernel(offsets, fractions, coefs, main, out, grid, once, twice):
    rows = main.shape[1]

    def relay(start, size):
        for u in range(size):
            load(grid, start + u, main, start + u)

    first_step, second_step = two_steps(
        lambda step, at: offsets[step, at],
        lambda step, at: fractions[step, at],
        lambda at: coefs[at] * PER_DIFFERENCE,
        lambda i, c: grid[i, c],
        once,
        twice,
    )
    in_groups(rows, RELAY, relay)
    in_groups(rows - 2 * REACH, FIRST, first_step)
    for lo in range(HALO, rows - HALO, GROUP):
        second_step(lo - HALO, GROUP)
        write(lambda i: offsets[1, i + HALO], twice, lo - HALO, GROUP, out, lo)


def edge_kernel(offsets, fractions, coefs, before, after, main, given, out, grid, once, twice, table, sems):
    del given
    members, rows, width = main.shape
    steps, per = offsets.shape[0], width // LANES
    halos = (before, after)
    copies = [
        pltpu.make_async_copy(halo.at[pl.ds(HALO * per * members, TILE)], table.at[side], sems.at[side])
        for side, halo in enumerate(halos)
    ]
    for copy in copies:
        copy.start()
    for side in range(2):
        for r in range(2 * HALO):
            load(grid.at[side], r, main, r + side * (rows - 2 * HALO))

    def side_steps(side):
        def own(at):
            return at - HALO * (1 - side)

        def entry(mine, column, at):
            row = own(at)
            if 0 <= row < 2 * HALO:
                return mine(row + side * (rows - 2 * HALO))
            return table[side, at - 2 * HALO * side, column]

        def line(at, c):
            row = own(at)
            if 0 <= row < 2 * HALO:
                return grid[side, row, c]
            return halos[side][pl.ds(((at - 2 * HALO * side) * per + c) * members, members)]

        def offset(step, at):
            return entry(lambda row: offsets[step, row], step, at).astype(jnp.int32)

        def fraction(step, at):
            return entry(lambda row: fractions[step, row], steps + step, at)

        def factor(at):
            return entry(lambda row: coefs[row], 2 * steps, at) * PER_DIFFERENCE

        return offset, *two_steps(offset, fraction, factor, line, once.at[side], twice.at[side])

    sides = [side_steps(side) for side in range(2)]
    for side, (_, first_step, _) in enumerate(sides):
        first_step(REACH * (1 - side), HALO + REACH)
    for copy in copies:
        copy.wait()
    for side, (_, first_step, _) in enumerate(sides):
        first_step((HALO + REACH) * side, REACH)
    for _, _, second_step in sides:
        second_step(0, HALO)
    for side, (offset, _, _) in enumerate(sides):
        whole = functools.partial(offset, 1)
        write(lambda i, whole=whole: whole(i + HALO), twice.at[side], 0, HALO, out, side * (rows - HALO))


SMEM = pl.BlockSpec(memory_space=pltpu.SMEM)
VMEM = pl.BlockSpec(memory_space=pltpu.VMEM)


def grant(mebibytes):
    return pltpu.CompilerParams(vmem_limit_bytes=mebibytes << 20)


def edge_radii(offsets, fractions, coefs, main):
    members, _, width = main.shape
    side = jax.ShapeDtypeStruct((HALO * members * width // LANES + TILE, LANES), jnp.float32)
    return pl.pallas_call(
        edge_radii_kernel,
        out_shape=[side, side],
        in_specs=[SMEM] * 3 + [VMEM],
        out_specs=[VMEM, VMEM],
        compiler_params=grant(2),
    )(offsets, fractions, coefs, main)


def inner(offsets, fractions, coefs, main):
    members, rows, width = main.shape
    per = width // LANES
    return pl.pallas_call(
        inner_kernel,
        out_shape=pltpu.VMEM(main.shape, jnp.float32),
        in_specs=[SMEM] * 3 + [VMEM],
        out_specs=VMEM,
        scratch_shapes=[
            pltpu.VMEM((rows, per, members, LANES), jnp.float32),
            pltpu.VMEM((rows - 2 * REACH, per, 2 * members, LANES), jnp.float32),
            pltpu.VMEM((rows - 2 * HALO, per, 2 * members, LANES), jnp.float32),
        ],
        compiler_params=grant(16),
    )(offsets, fractions, coefs, main)


def edges(offsets, fractions, coefs, before, after, main, done):
    members, _, width = main.shape
    per = width // LANES
    return pl.pallas_call(
        edge_kernel,
        out_shape=pltpu.VMEM(main.shape, jnp.float32),
        in_specs=[SMEM] * 3 + [VMEM] * 4,
        out_specs=VMEM,
        scratch_shapes=[
            pltpu.VMEM((2, 2 * HALO, per, members, LANES), jnp.float32),
            pltpu.VMEM((2, HALO + 2 * REACH, per, 2 * members, LANES), jnp.float32),
            pltpu.VMEM((2, HALO, per, 2 * members, LANES), jnp.float32),
            pltpu.SMEM((2, TILE, LANES), jnp.float32),
            pltpu.SemaphoreType.DMA((2,)),
        ],
        input_output_aliases={6: 0},
        compiler_params=grant(6),
    )(offsets, fractions, coefs, before, after, main, pltpu.with_memory_space_constraint(done, pltpu.VMEM))


def owners(parts, members):
    half = members // 2
    return [[part * members + (m + part % 2 * half) % members for m in range(members)] for part in range(parts)]


def exchanged(blocks, devices):
    return lax.all_to_all(blocks, ("rad", "azi"), 0, 0, axis_index_groups=devices, tiled=True)


def from_neighbours(first, last, devices):
    forth = [pair for part, after in zip(devices, devices[1:] + devices[:1]) for pair in zip(part, after)]
    back = [(j, i) for i, j in forth]
    return lax.ppermute(last, ("rad", "azi"), forth), lax.ppermute(first, ("rad", "azi"), back)


def shards(fields, offsets, fractions, coefs):
    shape = fields.shape
    rows, width = shape[2], shape[3]
    blocks = fields.reshape(-1, rows, width)
    devices = owners(lax.axis_size("rad"), lax.axis_size("azi"))
    main = exchanged(blocks, devices)

    before, after = from_neighbours(*edge_radii(offsets, fractions, coefs, main), devices)
    done = inner(offsets, fractions, coefs, main)
    done = edges(offsets, fractions, coefs, before, after, main, done)
    return exchanged(done, devices).reshape(shape)


def solution(mesh):
    placed = (P(None, None, "rad", "azi"), P(None, "rad"), P(None, "rad"), P("rad"))
    return jax.shard_map(
        shards, mesh=mesh, in_specs=placed, out_specs=P(None, None, "rad", "azi"), check_vma=False
    )
```

```python
import functools

import jax
import jax.numpy as jnp
from jax import lax
from jax.experimental import pallas as pl
from jax.experimental.pallas import tpu as pltpu
from jax.sharding import PartitionSpec as P

LANES = 128
REACH = 2
HALO = 2 * REACH
PER_DIFFERENCE = 1.0 / 12.0
RELAY, FIRST, GROUP = 16, 60, 8


def diffused(far_up, up, here, down, far_down, factor):
    return here + factor * (16.0 * (up + down) - (far_up + far_down) - 30.0 * here)


def partly_shifted(row, shift, weight):
    part = shift & (LANES - 1)
    lane = lax.broadcasted_iota(jnp.int32, row[0].shape, 1)
    own_first, own_behind = lane >= part, lane > part
    first = [pltpu.roll(line, part, 1) for line in row]
    behind = [pltpu.roll(line, (part + 1) & (LANES - 1), 1) for line in row]
    first = [pltpu.roll(first[-1], 1, 0)] + first
    behind = [pltpu.roll(behind[-1], 1, 0)] + behind
    return [
        (1.0 - weight) * jnp.where(own_first, first[c + 1], first[c])
        + weight * jnp.where(own_behind, behind[c + 1], behind[c])
        for c in range(len(row))
    ]


def keep(ref, i, row):
    blocks = row[0].shape[0]
    for c, line in enumerate(row):
        ref[i, c, pl.ds(0, blocks)] = line
        ref[i, c, pl.ds(blocks, blocks)] = line


def moved_line(ref, i, shift, c):
    per, blocks = ref.shape[1], ref.shape[2] // 2
    lines = shift >> 7
    some, whole = lines & (per - 1), lines >> (per.bit_length() - 1)
    wraps = (c < some).astype(jnp.int32)
    return ref[i, c - some + wraps * per, pl.ds(blocks - whole - wraps, blocks)]


def moved(ref, i, shift):
    return [moved_line(ref, i, shift, c) for c in range(ref.shape[1])]


def in_groups(count, size, body):
    size = next(s for s in range(size, 0, -1) if count % s == 0)

    def group(t, carry):
        body(t * size, size)
        return carry

    lax.fori_loop(0, count // size, group, 0)


def two_steps(offset, fraction, factor, grid, once, twice):
    per = grid.shape[1]

    def diffuse(start, size, at, number, line, out):
        rows = [[] for _ in range(size)]
        for c in range(per):
            read = [line(start + j, c) for j in range(size + 2 * REACH)]
            for u in range(size):
                rows[u].append(diffused(*read[u : u + 2 * REACH + 1], factor(start + u + at)))
        for u in range(size):
            here = start + u + at
            keep(out, start + u, partly_shifted(rows[u], offset(number, here), fraction(number, here)))

    def first_step(start, size):
        diffuse(start, size, REACH, 0, lambda i, c: grid[i, c], once)

    def second_step(start, size):
        diffuse(start, size, HALO, 1, lambda i, c: moved_line(once, i, offset(0, i + REACH), c), twice)

    return first_step, second_step


def write(offset, twice, start, count, out, to):
    for i in range(count):
        out[:, to + i, :] = jnp.concatenate(moved(twice, start + i, offset(start + i)), axis=1)


def load(grid, at, source, row, turn=0):
    line = source[pl.ds(0, grid.shape[2]), row, :]
    if turn:
        line = jnp.concatenate([line[turn:], line[:turn]])
    for c in range(grid.shape[1]):
        grid[at, c] = line[:, c * LANES : (c + 1) * LANES]


def by_parity(even, odd):
    parity = lax.axis_index("rad") & 1
    pl.when(parity == 0)(even)
    pl.when(parity == 1)(odd)


def edge_radii_kernel(offsets, fractions, coefs, main, one, two):
    members, rows, width = main.shape
    steps = offsets.shape[0]
    part, parts = lax.axis_index("rad"), lax.axis_size("rad")
    lane = lax.broadcasted_iota(jnp.int32, (1, width), 1)

    def fill(out, start, sent):
        radii = main[:, start : start + HALO]
        out[pl.ds(0, members)] = jnp.where(sent, radii, jnp.zeros_like(radii))
        for r in range(HALO):
            at = start + r
            entries = [offsets[step, at].astype(jnp.float32) for step in range(steps)]
            entries += [fractions[step, at] for step in range(steps)]
            entries.append(coefs[at])
            line = jnp.zeros((1, width), jnp.float32)
            for column, entry in enumerate(entries):
                line = jnp.where(lane == column, jnp.where(sent, entry, 0.0), line)
            out[members, pl.ds(r, 1)] = line

    def fill_both(first, last):
        fill(first, 0, part > 0)
        fill(last, rows - HALO, part < parts - 1)

    by_parity(lambda: fill_both(two, one), lambda: fill_both(one, two))


def inner_kernel(offsets, fractions, coefs, main, out, grid, once, twice):
    rows = main.shape[1]

    def relay(start, size):
        for u in range(size):
            load(grid, start + u, main, start + u)

    first_step, second_step = two_steps(
        lambda step, at: offsets[step, at],
        lambda step, at: fractions[step, at],
        lambda at: coefs[at] * PER_DIFFERENCE,
        grid,
        once,
        twice,
    )
    in_groups(rows, RELAY, relay)
    in_groups(rows - 2 * REACH, FIRST, first_step)
    for lo in range(HALO, rows - HALO, GROUP):
        second_step(lo - HALO, GROUP)
        write(lambda i: offsets[1, i + HALO], twice, lo - HALO, GROUP, out, lo)


def edge_kernel(offsets, fractions, coefs, one, two, main, given, out, grid, once, twice, table, sems):
    del given
    members, rows, _ = main.shape
    steps = offsets.shape[0]

    def table_copy(side, halo):
        return pltpu.make_async_copy(halo.at[members, :, pl.ds(0, LANES)], table.at[side], sems.at[side])

    def take(before, after):
        halos = (before, after)
        for side, halo in enumerate(halos):
            table_copy(side, halo).start()
        for side, halo in enumerate(halos):
            for r in range(HALO):
                load(grid.at[side], r + side * 2 * HALO, halo, r, members // 2)

    by_parity(lambda: take(two, one), lambda: take(one, two))
    for side in range(2):
        for r in range(2 * HALO):
            load(grid.at[side], r + (1 - side) * HALO, main, r + side * (rows - 2 * HALO))
    for side in range(2):
        table_copy(side, one).wait()

    def side_steps(side):
        def entry(own, column, at):
            row = at - HALO if side == 0 else at + rows - 2 * HALO
            if 0 <= row < rows:
                return own(row)
            return table[side, row + HALO if side == 0 else row - rows, column]

        def offset(step, at):
            return entry(lambda row: offsets[step, row], step, at).astype(jnp.int32)

        def fraction(step, at):
            return entry(lambda row: fractions[step, row], steps + step, at)

        def factor(at):
            return entry(lambda row: coefs[row], 2 * steps, at) * PER_DIFFERENCE

        first_step, second_step = two_steps(offset, fraction, factor, grid.at[side], once.at[side], twice.at[side])
        return offset, first_step, second_step

    sides = [side_steps(side) for side in range(2)]
    for _, first_step, _ in sides:
        first_step(0, HALO + 2 * REACH)
    for _, _, second_step in sides:
        second_step(0, HALO)
    for side, (offset, _, _) in enumerate(sides):
        whole = functools.partial(offset, 1)
        write(lambda i, whole=whole: whole(i + HALO), twice.at[side], 0, HALO, out, side * (rows - HALO))


SMEM = pl.BlockSpec(memory_space=pltpu.SMEM)
VMEM = pl.BlockSpec(memory_space=pltpu.VMEM)


def grant(mebibytes):
    return pltpu.CompilerParams(vmem_limit_bytes=mebibytes << 20)


def edge_radii(offsets, fractions, coefs, main):
    members, _, width = main.shape
    side = jax.ShapeDtypeStruct((members + 1, HALO, width), jnp.float32)
    return pl.pallas_call(
        edge_radii_kernel,
        out_shape=[side, side],
        in_specs=[SMEM] * 3 + [VMEM],
        out_specs=[VMEM, VMEM],
        compiler_params=grant(2),
    )(offsets, fractions, coefs, main)


def inner(offsets, fractions, coefs, main):
    members, rows, width = main.shape
    per = width // LANES
    return pl.pallas_call(
        inner_kernel,
        out_shape=pltpu.VMEM(main.shape, jnp.float32),
        in_specs=[SMEM] * 3 + [VMEM],
        out_specs=VMEM,
        scratch_shapes=[
            pltpu.VMEM((rows, per, members, LANES), jnp.float32),
            pltpu.VMEM((rows - 2 * REACH, per, 2 * members, LANES), jnp.float32),
            pltpu.VMEM((rows - 2 * HALO, per, 2 * members, LANES), jnp.float32),
        ],
        compiler_params=grant(16),
    )(offsets, fractions, coefs, main)


def edges(offsets, fractions, coefs, one, two, main, done):
    members, _, width = main.shape
    per = width // LANES
    return pl.pallas_call(
        edge_kernel,
        out_shape=pltpu.VMEM(main.shape, jnp.float32),
        in_specs=[SMEM] * 3 + [VMEM] * 4,
        out_specs=VMEM,
        scratch_shapes=[
            pltpu.VMEM((2, 3 * HALO, per, members, LANES), jnp.float32),
            pltpu.VMEM((2, HALO + 2 * REACH, per, 2 * members, LANES), jnp.float32),
            pltpu.VMEM((2, HALO, per, 2 * members, LANES), jnp.float32),
            pltpu.SMEM((2, HALO, LANES), jnp.float32),
            pltpu.SemaphoreType.DMA((2,)),
        ],
        input_output_aliases={6: 0},
        compiler_params=grant(6),
    )(offsets, fractions, coefs, one, two, main, pltpu.with_memory_space_constraint(done, pltpu.VMEM))


def owners(parts, members):
    half = members // 2
    return [[part * members + (m + part % 2 * half) % members for m in range(members)] for part in range(parts)]


def exchanged(blocks, devices):
    return lax.all_to_all(blocks, ("rad", "azi"), 0, 0, axis_index_groups=devices, tiled=True)


def swapped(one, two, devices):
    after = devices[1:] + devices[:1]

    def partners(start):
        pairs = [pair for a, b in zip(devices[start::2], after[start::2]) for pair in zip(a, b)]
        return pairs + [(b, a) for a, b in pairs]

    return lax.ppermute(one, ("rad", "azi"), partners(0)), lax.ppermute(two, ("rad", "azi"), partners(1))


def shards(fields, offsets, fractions, coefs):
    shape = fields.shape
    rows, width = shape[2], shape[3]
    blocks = fields.reshape(-1, rows, width)
    devices = owners(lax.axis_size("rad"), lax.axis_size("azi"))
    main = exchanged(blocks, devices)

    one, two = swapped(*edge_radii(offsets, fractions, coefs, main), devices)
    done = inner(offsets, fractions, coefs, main)
    done = edges(offsets, fractions, coefs, one, two, main, done)
    return exchanged(done, devices).reshape(shape)


def solution(mesh):
    placed = (P(None, None, "rad", "azi"), P(None, "rad"), P(None, "rad"), P("rad"))
    return jax.shard_map(
        shards, mesh=mesh, in_specs=placed, out_specs=P(None, None, "rad", "azi"), check_vma=False
    )
```

```python
import functools

import jax
import jax.numpy as jnp
from jax import lax
from jax.experimental import pallas as pl
from jax.experimental.pallas import tpu as pltpu
from jax.sharding import PartitionSpec as P

LANES = 128
REACH = 2
HALO = 2 * REACH
PER_DIFFERENCE = 1.0 / 12.0
TILE = 8
RELAY, FIRST, GROUP = 16, 60, 8


def diffused(far_up, up, here, down, far_down, factor):
    return here + factor * (16.0 * (up + down) - (far_up + far_down) - 30.0 * here)


def partly_shifted(row, shift, weight):
    part = shift & (LANES - 1)
    lane = lax.broadcasted_iota(jnp.int32, row[0].shape, 1)
    own_first, own_behind = lane >= part, lane > part
    first = [pltpu.roll(line, part, 1) for line in row]
    behind = [pltpu.roll(line, (part + 1) & (LANES - 1), 1) for line in row]
    first = [pltpu.roll(first[-1], 1, 0)] + first
    behind = [pltpu.roll(behind[-1], 1, 0)] + behind
    return [
        (1.0 - weight) * jnp.where(own_first, first[c + 1], first[c])
        + weight * jnp.where(own_behind, behind[c + 1], behind[c])
        for c in range(len(row))
    ]


def keep(ref, i, row):
    blocks = row[0].shape[0]
    for c, line in enumerate(row):
        ref[i, c, pl.ds(0, blocks)] = line
        ref[i, c, pl.ds(blocks, blocks)] = line


def moved_line(ref, i, shift, c):
    per, blocks = ref.shape[1], ref.shape[2] // 2
    lines = shift >> 7
    some, whole = lines & (per - 1), lines >> (per.bit_length() - 1)
    wraps = (c < some).astype(jnp.int32)
    return ref[i, c - some + wraps * per, pl.ds(blocks - whole - wraps, blocks)]


def moved(ref, i, shift):
    return [moved_line(ref, i, shift, c) for c in range(ref.shape[1])]


def in_groups(count, size, body):
    size = next(s for s in range(size, 0, -1) if count % s == 0)

    def group(t, carry):
        body(t * size, size)
        return carry

    lax.fori_loop(0, count // size, group, 0)


def two_steps(offset, fraction, factor, line, once, twice, kept):
    per = once.shape[1]

    def diffuse(start, size, at, number, line, out):
        rows = [[] for _ in range(size)]
        for c in range(per):
            read = [line(start + j, c) for j in range(size + 2 * REACH)]
            for u in range(size):
                rows[u].append(diffused(*read[u : u + 2 * REACH + 1], factor(start + u + at)))
        for u in range(size):
            here = start + u + at
            keep(out, start + u, partly_shifted(rows[u], offset(number, here), fraction(number, here)))

    def first_step(start, size):
        diffuse(start, size, REACH, 0, line, once)

    def second_step(start, size):
        diffuse(start, size, HALO, 1, lambda i, c: moved_line(*kept(i), offset(0, i + REACH), c), twice)

    return first_step, second_step


def write(offset, twice, start, count, out, to):
    for i in range(count):
        out[:, to + i, :] = jnp.concatenate(moved(twice, start + i, offset(start + i)), axis=1)


def load(grid, at, source, row):
    line = source[:, row, :]
    for c in range(grid.shape[1]):
        grid[at, c] = line[:, c * LANES : (c + 1) * LANES]


def edge_radii_kernel(offsets, fractions, coefs, main, first, last):
    members, rows, width = main.shape
    steps, per, half = offsets.shape[0], width // LANES, members // 2
    part, parts = lax.axis_index("rad"), lax.axis_size("rad")
    lane = lax.broadcasted_iota(jnp.int32, (1, LANES), 1)
    for out, start, sent in ((first, 0, part > 0), (last, rows - HALO, part < parts - 1)):
        for r in range(HALO):
            radius = main[:, start + r, :]
            radius = jnp.concatenate([radius[half:], radius[:half]])
            radius = jnp.where(sent, radius, jnp.zeros_like(radius))
            for c in range(per):
                out[pl.ds((r * per + c) * members, members)] = radius[:, c * LANES : (c + 1) * LANES]
        table = HALO * per * members
        out[pl.ds(table, TILE)] = jnp.zeros((TILE, LANES), jnp.float32)
        for r in range(HALO):
            at = start + r
            entries = [offsets[step, at].astype(jnp.float32) for step in range(steps)]
            entries += [fractions[step, at] for step in range(steps)]
            entries.append(coefs[at])
            line = jnp.zeros((1, LANES), jnp.float32)
            for column, entry in enumerate(entries):
                line = jnp.where(lane == column, jnp.where(sent, entry, 0.0), line)
            out[pl.ds(table + r, 1)] = line


def inner_kernel(offsets, fractions, coefs, main, out, near, stepped, grid, once, twice):
    rows = main.shape[1]

    def relay(start, size):
        for u in range(size):
            load(grid, start + u, main, start + u)

    first_step, second_step = two_steps(
        lambda step, at: offsets[step, at],
        lambda step, at: fractions[step, at],
        lambda at: coefs[at] * PER_DIFFERENCE,
        lambda i, c: grid[i, c],
        once,
        twice,
        lambda i: (once, i),
    )
    in_groups(rows, RELAY, relay)
    for r in range(HALO):
        near[0, r] = grid[r]
        near[1, r] = grid[rows - HALO + r]
    in_groups(rows - 2 * REACH, FIRST, first_step)
    for r in range(HALO):
        stepped[0, r] = once[r]
        stepped[1, r] = once[rows - 2 * REACH - HALO + r]
    for lo in range(HALO, rows - HALO, GROUP):
        second_step(lo - HALO, GROUP)
        write(lambda i: offsets[1, i + HALO], twice, lo - HALO, GROUP, out, lo)


def edge_kernel(offsets, fractions, coefs, before, after, near, stepped, given, out, once, twice, table, sems):
    del given
    members, rows, width = out.shape
    steps, per = offsets.shape[0], width // LANES
    halos = (before, after)
    copies = [
        pltpu.make_async_copy(halo.at[pl.ds(HALO * per * members, TILE)], table.at[side], sems.at[side])
        for side, halo in enumerate(halos)
    ]
    for copy in copies:
        copy.start()

    def side_steps(side):
        def own(at):
            return at - HALO * (1 - side)

        def entry(mine, column, at):
            row = own(at)
            if 0 <= row < 2 * HALO:
                return mine(row + side * (rows - 2 * HALO))
            return table[side, at - 2 * HALO * side, column]

        def line(at, c):
            row = own(at)
            if 0 <= row < 2 * HALO:
                return near[side, row - side * HALO, c]
            return halos[side][pl.ds(((at - 2 * HALO * side) * per + c) * members, members)]

        def kept(i):
            inward = i >= HALO if side == 0 else i < HALO
            return (stepped.at[side], i % HALO) if inward else (once.at[side], i)

        def offset(step, at):
            return entry(lambda row: offsets[step, row], step, at).astype(jnp.int32)

        def fraction(step, at):
            return entry(lambda row: fractions[step, row], steps + step, at)

        def factor(at):
            return entry(lambda row: coefs[row], 2 * steps, at) * PER_DIFFERENCE

        return offset, *two_steps(offset, fraction, factor, line, once.at[side], twice.at[side], kept)

    sides = [side_steps(side) for side in range(2)]
    for copy in copies:
        copy.wait()
    for side, (_, first_step, _) in enumerate(sides):
        first_step(side * HALO, HALO)
    for _, _, second_step in sides:
        second_step(0, HALO)
    for side, (offset, _, _) in enumerate(sides):
        whole = functools.partial(offset, 1)
        write(lambda i, whole=whole: whole(i + HALO), twice.at[side], 0, HALO, out, side * (rows - HALO))


SMEM = pl.BlockSpec(memory_space=pltpu.SMEM)
VMEM = pl.BlockSpec(memory_space=pltpu.VMEM)


def grant(mebibytes):
    return pltpu.CompilerParams(vmem_limit_bytes=mebibytes << 20)


def edge_radii(offsets, fractions, coefs, main):
    members, _, width = main.shape
    side = jax.ShapeDtypeStruct((HALO * members * width // LANES + TILE, LANES), jnp.float32)
    return pl.pallas_call(
        edge_radii_kernel,
        out_shape=[side, side],
        in_specs=[SMEM] * 3 + [VMEM],
        out_specs=[VMEM, VMEM],
        compiler_params=grant(2),
    )(offsets, fractions, coefs, main)


def inner(offsets, fractions, coefs, main):
    members, rows, width = main.shape
    per = width // LANES
    return pl.pallas_call(
        inner_kernel,
        out_shape=[
            pltpu.VMEM(main.shape, jnp.float32),
            pltpu.VMEM((2, HALO, per, members, LANES), jnp.float32),
            pltpu.VMEM((2, HALO, per, 2 * members, LANES), jnp.float32),
        ],
        in_specs=[SMEM] * 3 + [VMEM],
        out_specs=[VMEM] * 3,
        scratch_shapes=[
            pltpu.VMEM((rows, per, members, LANES), jnp.float32),
            pltpu.VMEM((rows - 2 * REACH, per, 2 * members, LANES), jnp.float32),
            pltpu.VMEM((rows - 2 * HALO, per, 2 * members, LANES), jnp.float32),
        ],
        compiler_params=grant(16),
    )(offsets, fractions, coefs, main)


def edges(offsets, fractions, coefs, before, after, done, near, stepped):
    members, _, width = done.shape
    per = width // LANES
    near, stepped, done = (pltpu.with_memory_space_constraint(part, pltpu.VMEM) for part in (near, stepped, done))
    return pl.pallas_call(
        edge_kernel,
        out_shape=pltpu.VMEM(done.shape, jnp.float32),
        in_specs=[SMEM] * 3 + [VMEM] * 5,
        out_specs=VMEM,
        scratch_shapes=[
            pltpu.VMEM((2, HALO + 2 * REACH, per, 2 * members, LANES), jnp.float32),
            pltpu.VMEM((2, HALO, per, 2 * members, LANES), jnp.float32),
            pltpu.SMEM((2, TILE, LANES), jnp.float32),
            pltpu.SemaphoreType.DMA((2,)),
        ],
        input_output_aliases={7: 0},
        compiler_params=grant(6),
    )(offsets, fractions, coefs, before, after, near, stepped, done)


def owners(parts, members):
    half = members // 2
    return [[part * members + (m + part % 2 * half) % members for m in range(members)] for part in range(parts)]


def exchanged(blocks, devices):
    return lax.all_to_all(blocks, ("rad", "azi"), 0, 0, axis_index_groups=devices, tiled=True)


def from_neighbours(first, last, devices):
    forth = [pair for part, after in zip(devices, devices[1:] + devices[:1]) for pair in zip(part, after)]
    back = [(j, i) for i, j in forth]
    return lax.ppermute(last, ("rad", "azi"), forth), lax.ppermute(first, ("rad", "azi"), back)


def shards(fields, offsets, fractions, coefs):
    shape = fields.shape
    rows, width = shape[2], shape[3]
    blocks = fields.reshape(-1, rows, width)
    devices = owners(lax.axis_size("rad"), lax.axis_size("azi"))
    main = exchanged(blocks, devices)

    before, after = from_neighbours(*edge_radii(offsets, fractions, coefs, main), devices)
    done = inner(offsets, fractions, coefs, main)
    done = edges(offsets, fractions, coefs, before, after, *done)
    return exchanged(done, devices).reshape(shape)


def solution(mesh):
    placed = (P(None, None, "rad", "azi"), P(None, "rad"), P(None, "rad"), P("rad"))
    return jax.shard_map(
        shards, mesh=mesh, in_specs=placed, out_specs=P(None, None, "rad", "azi"), check_vma=False
    )
```

```python
import functools

import jax
import jax.numpy as jnp
from jax import lax
from jax.experimental import pallas as pl
from jax.experimental.pallas import tpu as pltpu
from jax.sharding import PartitionSpec as P

LANES = 128
REACH = 2
HALO = 2 * REACH
PER_DIFFERENCE = 1.0 / 12.0
TILE = 8
RELAY, FIRST, GROUP = 16, 60, 8


def diffused(far_up, up, here, down, far_down, factor):
    return here + factor * (16.0 * (up + down) - (far_up + far_down) - 30.0 * here)


def partly_shifted(row, shift, weight):
    part = shift & (LANES - 1)
    lane = lax.broadcasted_iota(jnp.int32, row[0].shape, 1)
    own_first, own_behind = lane >= part, lane > part
    first = [pltpu.roll(line, part, 1) for line in row]
    behind = [pltpu.roll(line, (part + 1) & (LANES - 1), 1) for line in row]
    first = [pltpu.roll(first[-1], 1, 0)] + first
    behind = [pltpu.roll(behind[-1], 1, 0)] + behind
    return [
        (1.0 - weight) * jnp.where(own_first, first[c + 1], first[c])
        + weight * jnp.where(own_behind, behind[c + 1], behind[c])
        for c in range(len(row))
    ]


def keep(ref, i, row):
    blocks = row[0].shape[0]
    for c, line in enumerate(row):
        ref[i, c, pl.ds(0, blocks)] = line
        ref[i, c, pl.ds(blocks, blocks)] = line


def moved_line(ref, i, shift, c):
    per, blocks = ref.shape[1], ref.shape[2] // 2
    lines = shift >> 7
    some, whole = lines & (per - 1), lines >> (per.bit_length() - 1)
    wraps = (c < some).astype(jnp.int32)
    return ref[i, c - some + wraps * per, pl.ds(blocks - whole - wraps, blocks)]


def moved(ref, i, shift):
    return [moved_line(ref, i, shift, c) for c in range(ref.shape[1])]


def in_groups(count, size, body):
    size = next(s for s in range(size, 0, -1) if count % s == 0)

    def group(t, carry):
        body(t * size, size)
        return carry

    lax.fori_loop(0, count // size, group, 0)


def two_steps(offset, fraction, factor, line, once, twice, kept):
    per = once.shape[1]

    def diffuse(start, size, at, number, line, out):
        rows = [[] for _ in range(size)]
        for c in range(per):
            read = [line(start + j, c) for j in range(size + 2 * REACH)]
            for u in range(size):
                rows[u].append(diffused(*read[u : u + 2 * REACH + 1], factor(start + u + at)))
        for u in range(size):
            here = start + u + at
            keep(out, start + u, partly_shifted(rows[u], offset(number, here), fraction(number, here)))

    def first_step(start, size):
        diffuse(start, size, REACH, 0, line, once)

    def second_step(start, size):
        diffuse(start, size, HALO, 1, lambda i, c: moved_line(*kept(i), offset(0, i + REACH), c), twice)

    return first_step, second_step


def write(offset, twice, start, count, out, to):
    for i in range(count):
        out[:, to + i, :] = jnp.concatenate(moved(twice, start + i, offset(start + i)), axis=1)


def load(grid, at, source, row):
    line = source[:, row, :]
    for c in range(grid.shape[1]):
        grid[at, c] = line[:, c * LANES : (c + 1) * LANES]


def edge_radii_kernel(offsets, fractions, coefs, main, first, last):
    members, rows, width = main.shape
    steps, per, half = offsets.shape[0], width // LANES, members // 2
    part, parts = lax.axis_index("rad"), lax.axis_size("rad")
    lane = lax.broadcasted_iota(jnp.int32, (1, LANES), 1)
    for out, start, sent in ((first, 0, part > 0), (last, rows - HALO, part < parts - 1)):
        for r in range(HALO):
            radius = main[:, start + r, :]
            radius = jnp.concatenate([radius[half:], radius[:half]])
            radius = jnp.where(sent, radius, jnp.zeros_like(radius))
            for c in range(per):
                out[pl.ds((r * per + c) * members, members)] = radius[:, c * LANES : (c + 1) * LANES]
        table = HALO * per * members
        out[pl.ds(table, TILE)] = jnp.zeros((TILE, LANES), jnp.float32)
        for r in range(HALO):
            at = start + r
            entries = [offsets[step, at].astype(jnp.float32) for step in range(steps)]
            entries += [fractions[step, at] for step in range(steps)]
            entries.append(coefs[at])
            line = jnp.zeros((1, LANES), jnp.float32)
            for column, entry in enumerate(entries):
                line = jnp.where(lane == column, jnp.where(sent, entry, 0.0), line)
            out[pl.ds(table + r, 1)] = line


def inner_kernel(offsets, fractions, coefs, main, out, near, stepped, grid, once, twice):
    rows = main.shape[1]

    def relay(start, size):
        for u in range(size):
            load(grid, start + u, main, start + u)

    first_step, second_step = two_steps(
        lambda step, at: offsets[step, at],
        lambda step, at: fractions[step, at],
        lambda at: coefs[at] * PER_DIFFERENCE,
        lambda i, c: grid[i, c],
        once,
        twice,
        lambda i: (once, i),
    )
    in_groups(rows, RELAY, relay)
    for r in range(HALO):
        near[0, r] = grid[r]
        near[1, r] = grid[rows - HALO + r]
    in_groups(rows - 2 * REACH, FIRST, first_step)
    for r in range(HALO):
        stepped[0, r] = once[r]
        stepped[1, r] = once[rows - 2 * REACH - HALO + r]
    for lo in range(HALO, rows - HALO, GROUP):
        second_step(lo - HALO, GROUP)
        write(lambda i: offsets[1, i + HALO], twice, lo - HALO, GROUP, out, lo)


def edge_kernel(offsets, fractions, coefs, before, after, near, stepped, given, out, once, twice):
    del given
    members, rows, width = out.shape
    steps, per = offsets.shape[0], width // LANES
    halos = (before, after)
    tables = [halo[pl.ds(HALO * per * members, TILE)] for halo in halos]

    def side_steps(side):
        def own(at):
            return at - HALO * (1 - side)

        taken = {}

        def entry(mine, column, at):
            row = own(at)
            if 0 <= row < 2 * HALO:
                return mine(row + side * (rows - 2 * HALO))
            if (column, at) not in taken:
                taken[column, at] = tables[side][at - 2 * HALO * side, column]
            return taken[column, at]

        def line(at, c):
            row = own(at)
            if 0 <= row < 2 * HALO:
                return near[side, row - side * HALO, c]
            return halos[side][pl.ds(((at - 2 * HALO * side) * per + c) * members, members)]

        def kept(i):
            inward = i >= HALO if side == 0 else i < HALO
            return (stepped.at[side], i % HALO) if inward else (once.at[side], i)

        def offset(step, at):
            return entry(lambda row: offsets[step, row], step, at).astype(jnp.int32)

        def fraction(step, at):
            return entry(lambda row: fractions[step, row], steps + step, at)

        def factor(at):
            return entry(lambda row: coefs[row], 2 * steps, at) * PER_DIFFERENCE

        return offset, *two_steps(offset, fraction, factor, line, once.at[side], twice.at[side], kept)

    sides = [side_steps(side) for side in range(2)]
    for side, (_, first_step, _) in enumerate(sides):
        first_step(side * HALO, HALO)
    for _, _, second_step in sides:
        second_step(0, HALO)
    for side, (offset, _, _) in enumerate(sides):
        whole = functools.partial(offset, 1)
        write(lambda i, whole=whole: whole(i + HALO), twice.at[side], 0, HALO, out, side * (rows - HALO))


SMEM = pl.BlockSpec(memory_space=pltpu.SMEM)
VMEM = pl.BlockSpec(memory_space=pltpu.VMEM)


def grant(mebibytes):
    return pltpu.CompilerParams(vmem_limit_bytes=mebibytes << 20)


def edge_radii(offsets, fractions, coefs, main):
    members, _, width = main.shape
    side = jax.ShapeDtypeStruct((HALO * members * width // LANES + TILE, LANES), jnp.float32)
    return pl.pallas_call(
        edge_radii_kernel,
        out_shape=[side, side],
        in_specs=[SMEM] * 3 + [VMEM],
        out_specs=[VMEM, VMEM],
        compiler_params=grant(2),
    )(offsets, fractions, coefs, main)


def inner(offsets, fractions, coefs, main):
    members, rows, width = main.shape
    per = width // LANES
    return pl.pallas_call(
        inner_kernel,
        out_shape=[
            pltpu.VMEM(main.shape, jnp.float32),
            pltpu.VMEM((2, HALO, per, members, LANES), jnp.float32),
            pltpu.VMEM((2, HALO, per, 2 * members, LANES), jnp.float32),
        ],
        in_specs=[SMEM] * 3 + [VMEM],
        out_specs=[VMEM] * 3,
        scratch_shapes=[
            pltpu.VMEM((rows, per, members, LANES), jnp.float32),
            pltpu.VMEM((rows - 2 * REACH, per, 2 * members, LANES), jnp.float32),
            pltpu.VMEM((rows - 2 * HALO, per, 2 * members, LANES), jnp.float32),
        ],
        compiler_params=grant(16),
    )(offsets, fractions, coefs, main)


def edges(offsets, fractions, coefs, before, after, done, near, stepped):
    members, _, width = done.shape
    per = width // LANES
    near, stepped, done = (pltpu.with_memory_space_constraint(part, pltpu.VMEM) for part in (near, stepped, done))
    return pl.pallas_call(
        edge_kernel,
        out_shape=pltpu.VMEM(done.shape, jnp.float32),
        in_specs=[SMEM] * 3 + [VMEM] * 5,
        out_specs=VMEM,
        scratch_shapes=[
            pltpu.VMEM((2, HALO + 2 * REACH, per, 2 * members, LANES), jnp.float32),
            pltpu.VMEM((2, HALO, per, 2 * members, LANES), jnp.float32),
        ],
        input_output_aliases={7: 0},
        compiler_params=grant(6),
    )(offsets, fractions, coefs, before, after, near, stepped, done)


def owners(parts, members):
    half = members // 2
    return [[part * members + (m + part % 2 * half) % members for m in range(members)] for part in range(parts)]


def exchanged(blocks, devices):
    return lax.all_to_all(blocks, ("rad", "azi"), 0, 0, axis_index_groups=devices, tiled=True)


def from_neighbours(first, last, devices):
    forth = [pair for part, after in zip(devices, devices[1:] + devices[:1]) for pair in zip(part, after)]
    back = [(j, i) for i, j in forth]
    return lax.ppermute(last, ("rad", "azi"), forth), lax.ppermute(first, ("rad", "azi"), back)


def shards(fields, offsets, fractions, coefs):
    shape = fields.shape
    rows, width = shape[2], shape[3]
    blocks = fields.reshape(-1, rows, width)
    devices = owners(lax.axis_size("rad"), lax.axis_size("azi"))
    main = exchanged(blocks, devices)

    before, after = from_neighbours(*edge_radii(offsets, fractions, coefs, main), devices)
    done = inner(offsets, fractions, coefs, main)
    done = edges(offsets, fractions, coefs, before, after, *done)
    return exchanged(done, devices).reshape(shape)


def solution(mesh):
    placed = (P(None, None, "rad", "azi"), P(None, "rad"), P(None, "rad"), P("rad"))
    return jax.shard_map(
        shards, mesh=mesh, in_specs=placed, out_specs=P(None, None, "rad", "azi"), check_vma=False
    )
```

```python
import functools

import jax
import jax.numpy as jnp
from jax import lax
from jax.experimental import pallas as pl
from jax.experimental.pallas import tpu as pltpu
from jax.sharding import PartitionSpec as P

LANES = 128
REACH = 2
HALO = 2 * REACH
PER_DIFFERENCE = 1.0 / 12.0
TILE = 8
RELAY, FIRST, GROUP = 16, 60, 8


def diffused(far_up, up, here, down, far_down, factor):
    return here + factor * (16.0 * (up + down) - (far_up + far_down) - 30.0 * here)


def partly_shifted(row, shift, weight):
    part = shift & (LANES - 1)
    lane = lax.broadcasted_iota(jnp.int32, row[0].shape, 1)
    own_first, own_behind = lane >= part, lane > part
    first = [pltpu.roll(line, part, 1) for line in row]
    behind = [pltpu.roll(line, (part + 1) & (LANES - 1), 1) for line in row]
    first = [pltpu.roll(first[-1], 1, 0)] + first
    behind = [pltpu.roll(behind[-1], 1, 0)] + behind
    return [
        (1.0 - weight) * jnp.where(own_first, first[c + 1], first[c])
        + weight * jnp.where(own_behind, behind[c + 1], behind[c])
        for c in range(len(row))
    ]


def keep(ref, i, row):
    blocks = row[0].shape[0]
    for c, line in enumerate(row):
        ref[i, c, pl.ds(0, blocks)] = line
        ref[i, c, pl.ds(blocks, blocks)] = line


def moved_line(ref, i, shift, c):
    per, blocks = ref.shape[1], ref.shape[2] // 2
    lines = shift >> 7
    some, whole = lines & (per - 1), lines >> (per.bit_length() - 1)
    wraps = (c < some).astype(jnp.int32)
    return ref[i, c - some + wraps * per, pl.ds(blocks - whole - wraps, blocks)]


def moved(ref, i, shift):
    return [moved_line(ref, i, shift, c) for c in range(ref.shape[1])]


def in_groups(count, size, body):
    size = next(s for s in range(size, 0, -1) if count % s == 0)

    def group(t, carry):
        body(t * size, size)
        return carry

    lax.fori_loop(0, count // size, group, 0)


def two_steps(offset, fraction, factor, line, once, twice, kept):
    per = once.shape[1]

    def diffuse(start, size, at, number, line, out):
        rows = [[] for _ in range(size)]
        for c in range(per):
            read = [line(start + j, c) for j in range(size + 2 * REACH)]
            for u in range(size):
                rows[u].append(diffused(*read[u : u + 2 * REACH + 1], factor(start + u + at)))
        for u in range(size):
            here = start + u + at
            keep(out, start + u, partly_shifted(rows[u], offset(number, here), fraction(number, here)))

    def first_step(start, size):
        diffuse(start, size, REACH, 0, line, once)

    def second_step(start, size):
        diffuse(start, size, HALO, 1, lambda i, c: moved_line(*kept(i), offset(0, i + REACH), c), twice)

    return first_step, second_step


def write(offset, twice, start, count, out, to):
    for i in range(count):
        out[:, to + i, :] = jnp.concatenate(moved(twice, start + i, offset(start + i)), axis=1)


def load(grid, at, source, row):
    line = source[:, row, :]
    for c in range(grid.shape[1]):
        grid[at, c] = line[:, c * LANES : (c + 1) * LANES]


def edge_radii_kernel(offsets, fractions, coefs, main, first, last):
    members, rows, width = main.shape
    per, half = width // LANES, members // 2
    part, parts = lax.axis_index("rad"), lax.axis_size("rad")
    for out, start, sent in ((first, 0, part > 0), (last, rows - HALO, part < parts - 1)):
        for r in range(HALO):
            radius = main[:, start + r, :]
            radius = jnp.concatenate([radius[half:], radius[:half]])
            radius = jnp.where(sent, radius, jnp.zeros_like(radius))
            for c in range(per):
                out[pl.ds((r * per + c) * members, members)] = radius[:, c * LANES : (c + 1) * LANES]
        at = HALO * per * members
        out[pl.ds(at, TILE)] = jnp.zeros((TILE, LANES), jnp.float32)
        for entries in (offsets[...].astype(jnp.float32), fractions[...], coefs[...]):
            count = entries.shape[0]
            out[pl.ds(at, count), pl.ds(0, rows)] = jnp.where(sent, entries, jnp.zeros_like(entries))
            at += count


def inner_kernel(offsets, fractions, coefs, main, out, near, stepped, grid, once, twice):
    rows = main.shape[1]

    def relay(start, size):
        for u in range(size):
            load(grid, start + u, main, start + u)

    first_step, second_step = two_steps(
        lambda step, at: offsets[step, at],
        lambda step, at: fractions[step, at],
        lambda at: coefs[at] * PER_DIFFERENCE,
        lambda i, c: grid[i, c],
        once,
        twice,
        lambda i: (once, i),
    )
    in_groups(rows, RELAY, relay)
    for r in range(HALO):
        near[0, r] = grid[r]
        near[1, r] = grid[rows - HALO + r]
    in_groups(rows - 2 * REACH, FIRST, first_step)
    for r in range(HALO):
        stepped[0, r] = once[r]
        stepped[1, r] = once[rows - 2 * REACH - HALO + r]
    for lo in range(HALO, rows - HALO, GROUP):
        second_step(lo - HALO, GROUP)
        write(lambda i: offsets[1, i + HALO], twice, lo - HALO, GROUP, out, lo)


def edge_kernel(offsets, fractions, coefs, before, after, near, stepped, given, out, once, twice):
    del given
    members, rows, width = out.shape
    steps, per = offsets.shape[0], width // LANES
    halos = (before, after)
    tables = [halo[pl.ds(HALO * per * members, TILE)] for halo in halos]

    def side_steps(side):
        def own(at):
            return at - HALO * (1 - side)

        taken = {}

        def entry(mine, column, at):
            row = own(at)
            if 0 <= row < 2 * HALO:
                return mine(row + side * (rows - 2 * HALO))
            if (column, at) not in taken:
                taken[column, at] = tables[side][column, at + (rows - HALO if side == 0 else -2 * HALO)]
            return taken[column, at]

        def line(at, c):
            row = own(at)
            if 0 <= row < 2 * HALO:
                return near[side, row - side * HALO, c]
            return halos[side][pl.ds(((at - 2 * HALO * side) * per + c) * members, members)]

        def kept(i):
            inward = i >= HALO if side == 0 else i < HALO
            return (stepped.at[side], i % HALO) if inward else (once.at[side], i)

        def offset(step, at):
            return entry(lambda row: offsets[step, row], step, at).astype(jnp.int32)

        def fraction(step, at):
            return entry(lambda row: fractions[step, row], steps + step, at)

        def factor(at):
            return entry(lambda row: coefs[row], 2 * steps, at) * PER_DIFFERENCE

        return offset, *two_steps(offset, fraction, factor, line, once.at[side], twice.at[side], kept)

    sides = [side_steps(side) for side in range(2)]
    for side, (_, first_step, _) in enumerate(sides):
        first_step(side * HALO, HALO)
    for _, _, second_step in sides:
        second_step(0, HALO)
    for side, (offset, _, _) in enumerate(sides):
        whole = functools.partial(offset, 1)
        write(lambda i, whole=whole: whole(i + HALO), twice.at[side], 0, HALO, out, side * (rows - HALO))


SMEM = pl.BlockSpec(memory_space=pltpu.SMEM)
VMEM = pl.BlockSpec(memory_space=pltpu.VMEM)


def grant(mebibytes):
    return pltpu.CompilerParams(vmem_limit_bytes=mebibytes << 20)


def edge_radii(offsets, fractions, coefs, main):
    members, _, width = main.shape
    side = jax.ShapeDtypeStruct((HALO * members * width // LANES + TILE, LANES), jnp.float32)
    return pl.pallas_call(
        edge_radii_kernel,
        out_shape=[side, side],
        in_specs=[VMEM] * 4,
        out_specs=[VMEM, VMEM],
        compiler_params=grant(2),
    )(offsets, fractions, coefs[None], main)


def inner(offsets, fractions, coefs, main):
    members, rows, width = main.shape
    per = width // LANES
    return pl.pallas_call(
        inner_kernel,
        out_shape=[
            pltpu.VMEM(main.shape, jnp.float32),
            pltpu.VMEM((2, HALO, per, members, LANES), jnp.float32),
            pltpu.VMEM((2, HALO, per, 2 * members, LANES), jnp.float32),
        ],
        in_specs=[SMEM] * 3 + [VMEM],
        out_specs=[VMEM] * 3,
        scratch_shapes=[
            pltpu.VMEM((rows, per, members, LANES), jnp.float32),
            pltpu.VMEM((rows - 2 * REACH, per, 2 * members, LANES), jnp.float32),
            pltpu.VMEM((rows - 2 * HALO, per, 2 * members, LANES), jnp.float32),
        ],
        compiler_params=grant(16),
    )(offsets, fractions, coefs, main)


def edges(offsets, fractions, coefs, before, after, done, near, stepped):
    members, _, width = done.shape
    per = width // LANES
    near, stepped, done = (pltpu.with_memory_space_constraint(part, pltpu.VMEM) for part in (near, stepped, done))
    return pl.pallas_call(
        edge_kernel,
        out_shape=pltpu.VMEM(done.shape, jnp.float32),
        in_specs=[SMEM] * 3 + [VMEM] * 5,
        out_specs=VMEM,
        scratch_shapes=[
            pltpu.VMEM((2, HALO + 2 * REACH, per, 2 * members, LANES), jnp.float32),
            pltpu.VMEM((2, HALO, per, 2 * members, LANES), jnp.float32),
        ],
        input_output_aliases={7: 0},
        compiler_params=grant(6),
    )(offsets, fractions, coefs, before, after, near, stepped, done)


def owners(parts, members):
    half = members // 2
    return [[part * members + (m + part % 2 * half) % members for m in range(members)] for part in range(parts)]


def exchanged(blocks, devices):
    return lax.all_to_all(blocks, ("rad", "azi"), 0, 0, axis_index_groups=devices, tiled=True)


def from_neighbours(first, last, devices):
    forth = [pair for part, after in zip(devices, devices[1:] + devices[:1]) for pair in zip(part, after)]
    back = [(j, i) for i, j in forth]
    return lax.ppermute(last, ("rad", "azi"), forth), lax.ppermute(first, ("rad", "azi"), back)


def shards(fields, offsets, fractions, coefs):
    shape = fields.shape
    rows, width = shape[2], shape[3]
    blocks = fields.reshape(-1, rows, width)
    devices = owners(lax.axis_size("rad"), lax.axis_size("azi"))
    main = exchanged(blocks, devices)

    before, after = from_neighbours(*edge_radii(offsets, fractions, coefs, main), devices)
    done = inner(offsets, fractions, coefs, main)
    done = edges(offsets, fractions, coefs, before, after, *done)
    return exchanged(done, devices).reshape(shape)


def solution(mesh):
    placed = (P(None, None, "rad", "azi"), P(None, "rad"), P(None, "rad"), P("rad"))
    return jax.shard_map(
        shards, mesh=mesh, in_specs=placed, out_specs=P(None, None, "rad", "azi"), check_vma=False
    )
```

```python
import functools

import jax
import jax.numpy as jnp
from jax import lax
from jax.experimental import pallas as pl
from jax.experimental.pallas import tpu as pltpu
from jax.sharding import PartitionSpec as P

LANES = 128
REACH = 2
HALO = 2 * REACH
PER_DIFFERENCE = 1.0 / 12.0
TILE = 8
RELAY, FIRST, GROUP = 16, 60, 8


def diffused(far_up, up, here, down, far_down, factor):
    return here + factor * (16.0 * (up + down) - (far_up + far_down) - 30.0 * here)


def partly_shifted(row, shift, weight):
    part = shift & (LANES - 1)
    lane = lax.broadcasted_iota(jnp.int32, row[0].shape, 1)
    own_first, own_behind = lane >= part, lane > part
    first = [pltpu.roll(line, part, 1) for line in row]
    behind = [pltpu.roll(line, (part + 1) & (LANES - 1), 1) for line in row]
    first = [pltpu.roll(first[-1], 1, 0)] + first
    behind = [pltpu.roll(behind[-1], 1, 0)] + behind
    return [
        (1.0 - weight) * jnp.where(own_first, first[c + 1], first[c])
        + weight * jnp.where(own_behind, behind[c + 1], behind[c])
        for c in range(len(row))
    ]


def keep(ref, i, row):
    blocks = row[0].shape[0]
    for c, line in enumerate(row):
        ref[i, c, pl.ds(0, blocks)] = line
        ref[i, c, pl.ds(blocks, blocks)] = line


def moved_line(ref, i, shift, c):
    per, blocks = ref.shape[1], ref.shape[2] // 2
    lines = shift >> 7
    some, whole = lines & (per - 1), lines >> (per.bit_length() - 1)
    wraps = (c < some).astype(jnp.int32)
    return ref[i, c - some + wraps * per, pl.ds(blocks - whole - wraps, blocks)]


def moved(ref, i, shift):
    return [moved_line(ref, i, shift, c) for c in range(ref.shape[1])]


def in_groups(count, size, body):
    size = next(s for s in range(size, 0, -1) if count % s == 0)

    def group(t, carry):
        body(t * size, size)
        return carry

    lax.fori_loop(0, count // size, group, 0)


def two_steps(offset, fraction, factor, line, once, twice, kept):
    per = once.shape[1]

    def diffuse(start, size, at, number, line, out):
        rows = [[] for _ in range(size)]
        for c in range(per):
            read = [line(start + j, c) for j in range(size + 2 * REACH)]
            for u in range(size):
                rows[u].append(diffused(*read[u : u + 2 * REACH + 1], factor(start + u + at)))
        for u in range(size):
            here = start + u + at
            keep(out, start + u, partly_shifted(rows[u], offset(number, here), fraction(number, here)))

    def first_step(start, size):
        diffuse(start, size, REACH, 0, line, once)

    def second_step(start, size):
        diffuse(start, size, HALO, 1, lambda i, c: moved_line(*kept(i), offset(0, i + REACH), c), twice)

    return first_step, second_step


def write(offset, twice, start, count, out, to):
    for i in range(count):
        out[:, to + i, :] = jnp.concatenate(moved(twice, start + i, offset(start + i)), axis=1)


def load(grid, at, source, row):
    line = source[:, row, :]
    for c in range(grid.shape[1]):
        grid[at, c] = line[:, c * LANES : (c + 1) * LANES]


def edge_radii_kernel(offsets, fractions, coefs, main, first, last):
    members, rows, width = main.shape
    per, half = width // LANES, members // 2
    part, parts = lax.axis_index("rad"), lax.axis_size("rad")
    for out, start, sent in ((first, 0, part > 0), (last, rows - HALO, part < parts - 1)):
        for r in range(HALO):
            radius = main[:, start + r, :]
            radius = jnp.concatenate([radius[half:], radius[:half]])
            radius = jnp.where(sent, radius, jnp.zeros_like(radius))
            for c in range(per):
                out[pl.ds((r * per + c) * members, members)] = radius[:, c * LANES : (c + 1) * LANES]
        at = HALO * per * members
        out[pl.ds(at, TILE)] = jnp.zeros((TILE, LANES), jnp.float32)
        for entries in (offsets[...].astype(jnp.float32), fractions[...], coefs[...]):
            count = entries.shape[0]
            out[pl.ds(at, count), pl.ds(0, rows)] = jnp.where(sent, entries, jnp.zeros_like(entries))
            at += count


def inner_kernel(offsets, fractions, coefs, main, out, near, stepped, grid, once, twice):
    rows = main.shape[1]

    def relay(start, size):
        for u in range(size):
            load(grid, start + u, main, start + u)

    first_step, second_step = two_steps(
        lambda step, at: offsets[step, at],
        lambda step, at: fractions[step, at],
        lambda at: coefs[at] * PER_DIFFERENCE,
        lambda i, c: grid[i, c],
        once,
        twice,
        lambda i: (once, i),
    )
    in_groups(rows, RELAY, relay)
    for r in range(HALO):
        near[0, r] = grid[r]
        near[1, r] = grid[rows - HALO + r]
    in_groups(rows - 2 * REACH, FIRST, first_step)
    for r in range(HALO):
        stepped[0, r] = once[r]
        stepped[1, r] = once[rows - 2 * REACH - HALO + r]
    for lo in range(HALO, rows - HALO, GROUP):
        second_step(lo - HALO, GROUP)
        write(lambda i: offsets[1, i + HALO], twice, lo - HALO, GROUP, out, lo)


def edge_kernel(offsets, fractions, coefs, before, after, near, stepped, given, out, once, twice):
    del given
    members, rows, width = out.shape
    steps, per = offsets.shape[0], width // LANES
    halos = (before, after)
    offsets, fractions, coefs = offsets[...], fractions[...], coefs[...]
    tables = [halo[pl.ds(HALO * per * members, TILE)] for halo in halos]

    def side_steps(side):
        def own(at):
            return at - HALO * (1 - side)

        taken = {}

        def entry(mine, column, at):
            row = own(at)
            if (column, at) in taken:
                return taken[column, at]
            if 0 <= row < 2 * HALO:
                taken[column, at] = mine(row + side * (rows - 2 * HALO))
            else:
                taken[column, at] = tables[side][column, at + (rows - HALO if side == 0 else -2 * HALO)]
            return taken[column, at]

        def line(at, c):
            row = own(at)
            if 0 <= row < 2 * HALO:
                return near[side, row - side * HALO, c]
            return halos[side][pl.ds(((at - 2 * HALO * side) * per + c) * members, members)]

        def kept(i):
            inward = i >= HALO if side == 0 else i < HALO
            return (stepped.at[side], i % HALO) if inward else (once.at[side], i)

        def offset(step, at):
            return entry(lambda row: offsets[step, row], step, at).astype(jnp.int32)

        def fraction(step, at):
            return entry(lambda row: fractions[step, row], steps + step, at)

        def factor(at):
            return entry(lambda row: coefs[0, row], 2 * steps, at) * PER_DIFFERENCE

        return offset, *two_steps(offset, fraction, factor, line, once.at[side], twice.at[side], kept)

    sides = [side_steps(side) for side in range(2)]
    for side, (_, first_step, _) in enumerate(sides):
        first_step(side * HALO, HALO)
    for _, _, second_step in sides:
        second_step(0, HALO)
    for side, (offset, _, _) in enumerate(sides):
        whole = functools.partial(offset, 1)
        write(lambda i, whole=whole: whole(i + HALO), twice.at[side], 0, HALO, out, side * (rows - HALO))


SMEM = pl.BlockSpec(memory_space=pltpu.SMEM)
VMEM = pl.BlockSpec(memory_space=pltpu.VMEM)


def grant(mebibytes):
    return pltpu.CompilerParams(vmem_limit_bytes=mebibytes << 20)


def edge_radii(offsets, fractions, coefs, main):
    members, _, width = main.shape
    side = jax.ShapeDtypeStruct((HALO * members * width // LANES + TILE, LANES), jnp.float32)
    return pl.pallas_call(
        edge_radii_kernel,
        out_shape=[side, side],
        in_specs=[VMEM] * 4,
        out_specs=[VMEM, VMEM],
        compiler_params=grant(2),
    )(offsets, fractions, coefs[None], main)


def inner(offsets, fractions, coefs, main):
    members, rows, width = main.shape
    per = width // LANES
    return pl.pallas_call(
        inner_kernel,
        out_shape=[
            pltpu.VMEM(main.shape, jnp.float32),
            pltpu.VMEM((2, HALO, per, members, LANES), jnp.float32),
            pltpu.VMEM((2, HALO, per, 2 * members, LANES), jnp.float32),
        ],
        in_specs=[SMEM] * 3 + [VMEM],
        out_specs=[VMEM] * 3,
        scratch_shapes=[
            pltpu.VMEM((rows, per, members, LANES), jnp.float32),
            pltpu.VMEM((rows - 2 * REACH, per, 2 * members, LANES), jnp.float32),
            pltpu.VMEM((rows - 2 * HALO, per, 2 * members, LANES), jnp.float32),
        ],
        compiler_params=grant(16),
    )(offsets, fractions, coefs, main)


def edges(offsets, fractions, coefs, before, after, done, near, stepped):
    members, _, width = done.shape
    per = width // LANES
    near, stepped, done = (pltpu.with_memory_space_constraint(part, pltpu.VMEM) for part in (near, stepped, done))
    return pl.pallas_call(
        edge_kernel,
        out_shape=pltpu.VMEM(done.shape, jnp.float32),
        in_specs=[VMEM] * 8,
        out_specs=VMEM,
        scratch_shapes=[
            pltpu.VMEM((2, HALO + 2 * REACH, per, 2 * members, LANES), jnp.float32),
            pltpu.VMEM((2, HALO, per, 2 * members, LANES), jnp.float32),
        ],
        input_output_aliases={7: 0},
        compiler_params=grant(6),
    )(offsets, fractions, coefs[None], before, after, near, stepped, done)


def owners(parts, members):
    half = members // 2
    return [[part * members + (m + part % 2 * half) % members for m in range(members)] for part in range(parts)]


def exchanged(blocks, devices):
    return lax.all_to_all(blocks, ("rad", "azi"), 0, 0, axis_index_groups=devices, tiled=True)


def from_neighbours(first, last, devices):
    forth = [pair for part, after in zip(devices, devices[1:] + devices[:1]) for pair in zip(part, after)]
    back = [(j, i) for i, j in forth]
    return lax.ppermute(last, ("rad", "azi"), forth), lax.ppermute(first, ("rad", "azi"), back)


def shards(fields, offsets, fractions, coefs):
    shape = fields.shape
    rows, width = shape[2], shape[3]
    blocks = fields.reshape(-1, rows, width)
    devices = owners(lax.axis_size("rad"), lax.axis_size("azi"))
    main = exchanged(blocks, devices)

    before, after = from_neighbours(*edge_radii(offsets, fractions, coefs, main), devices)
    done = inner(offsets, fractions, coefs, main)
    done = edges(offsets, fractions, coefs, before, after, *done)
    return exchanged(done, devices).reshape(shape)


def solution(mesh):
    placed = (P(None, None, "rad", "azi"), P(None, "rad"), P(None, "rad"), P("rad"))
    return jax.shard_map(
        shards, mesh=mesh, in_specs=placed, out_specs=P(None, None, "rad", "azi"), check_vma=False
    )
```
